32 devices in a mesh: kset: 2 (over y), grid: 16 (over z, x, core).
Axes of the slice: x: 2, y: 2, z: 4, core: 2. Of those that a mesh axis runs over, the one named last changes fastest.
Arguments:
- bands: bfloat16 [4, 4096, 1536], P('kset', 'grid'), parts along dimension 0, may hold values from -4 to 4, as said below
- hbands: bfloat16 [4, 4096, 1536], P('kset', 'grid'), parts along dimension 0, may hold values from -10 to 10, as said below
- occupied: int32 [4], P('kset'), parts along dimension 0, may hold values from 192 to 576
Outputs:
- new_bands: bfloat16 [4, 4096, 1536], P('kset', 'grid'), parts along dimension 0
The draws below stay inside these ranges and needn't reach their ends.
There are 2 independent parts, one for each index of `kset`. The reference program is written for one: setup_inputs(seed, part) draws one part's arguments, and reference() takes and returns one part's arrays. A program takes and returns all parts, laid end to end along the dimension named above; each array names one. Nothing has to cross between parts.
Inputs may be any that keep to these rules, and one draw needn't show every extreme that they name: `bands`: real values on every grid point. `hbands`: real values on every grid point.
All inputs are finite; a program needn't handle non-finite values.
Results may differ from the reference program's by a relative error of at most 0.0079.
Values may be sent and summed in bfloat16 or wider, within the bound.
A program may use at most 64 MiB of HBM per device.

```python
import math
import jax
import jax.numpy as jnp
from jax import lax

NB = 768
KP = 2
MCW = 2
GRID = 4096


def draw_pair(key):
    band_key = jax.random.fold_in(key, 11)
    noise_key = jax.random.fold_in(key, 12)
    shape = (KP, GRID, 2 * NB)
    base = jnp.clip(jax.random.normal(band_key, shape, jnp.float32), -4.0, 4.0)
    noise = jnp.clip(jax.random.normal(noise_key, shape, jnp.float32), -4.0, 4.0)
    column = jnp.arange(2 * NB) % NB
    energy = 1.0 + 2.0 * column.astype(jnp.float32) / NB
    factor = 1.4 * math.sqrt(NB / GRID)
    applied = jnp.clip(factor * energy * base + noise, -10.0, 10.0)
    return (base, applied)


def draw_bands(key, part):
    return draw_pair(key)[0].astype(jnp.bfloat16)


def draw_hbands(key, part):
    return draw_pair(key)[1].astype(jnp.bfloat16)


def setup_inputs(seed: int = 0, part: int = 0) -> dict:
    seeds = jax.random.split(jax.random.key(seed), 4)
    part_keys = jax.random.split(jax.random.fold_in(seeds[3], part), 4)
    bands = draw_bands(jax.random.fold_in(jax.random.fold_in(seeds[3], part), 71), part)
    hbands = draw_hbands(jax.random.fold_in(jax.random.fold_in(seeds[3], part), 71), part)
    occupied = jax.random.randint(part_keys[2], (KP,), NB // 4, 3 * NB // 4 + 1).astype(jnp.int32)
    return {"bands": bands, "hbands": hbands, "occupied": occupied}


def embedding(full):
    width = full.shape[-1] // 2
    real_part = full[..., :width]
    imag_part = full[..., width:]
    upper = jnp.concatenate([real_part, imag_part], -1)
    lower = jnp.concatenate([-imag_part, real_part], -1)
    return jnp.concatenate([upper, lower], -2)

def reference(bands, hbands, occupied):
    results = []
    for point in range(KP):
        band_f = bands[point].astype(jnp.float32)
        hband_f = hbands[point].astype(jnp.float32)
        product = jnp.dot(band_f.T, hband_f, precision=lax.Precision.HIGHEST)
        real_sum = product[:NB, :NB] + product[NB:, NB:]
        imag_sum = product[:NB, NB:] - product[NB:, :NB]
        ham_real = (real_sum + real_sum.T) / (2.0 * GRID)
        ham_imag = (imag_sum - imag_sum.T) / (2.0 * GRID)
        identity = jnp.eye(NB, dtype=jnp.float32)
        level = jnp.trace(ham_real) / NB
        centred = ham_real - level * identity
        total = jnp.sum(centred * centred) + jnp.sum(ham_imag * ham_imag)
        spread = jnp.sqrt(total / NB + 1e-06)
        filling = occupied[point].astype(jnp.float32) / NB
        dens_real = filling * identity - centred / (4.0 * spread)
        dens_imag = -ham_imag / (4.0 * spread)
        density = jnp.concatenate([dens_real, dens_imag], 1).astype(jnp.bfloat16)
        for repeat in range(MCW):
            matrix = embedding(density)
            square = jnp.dot(density, matrix, preferred_element_type=jnp.float32)
            cube = jnp.dot(square.astype(jnp.bfloat16), matrix, preferred_element_type=jnp.float32)
            density = (3.0 * square - 2.0 * cube).astype(jnp.bfloat16)
        matrix = embedding(density).astype(jnp.float32)
        updated = jnp.dot(band_f, matrix, precision=lax.Precision.HIGHEST)
        results.append(updated.astype(jnp.bfloat16))
    return jnp.stack(results)
```

```python
import functools

import jax
import jax.numpy as jnp
from jax import lax
from jax.experimental import pallas as pl
from jax.experimental.pallas import tpu as pltpu
from jax.sharding import PartitionSpec as P

MCW = 2
LINE = 4
CHIPS = 2 * LINE
TILE = 256
CHUNK = 128
PERIOD = 3
LAG = 2
MESH = pl.DeviceIdType.MESH


def dot_t(left, right):
    return lax.dot_general(
        left, right, (((0,), (0,)), ((), ())), preferred_element_type=jnp.float32
    )


def dot(left, right):
    return jnp.dot(left, right, preferred_element_type=jnp.float32)


def kernel(
    scale,
    occ_ref,
    bands_ref,
    hbands_ref,
    out_ref,
    mb,
    mh,
    rb,
    rh,
    packed,
    s1,
    r1,
    s2,
    r2,
    s3,
    r3,
    dl,
    dr,
    full,
    re0,
    im0,
    re1,
    im1,
    sr,
    si,
    ob,
    in_send,
    in_recv,
    ds_sem,
    dr_sem,
    c_send,
    c_recv,
    o_sem,
    load_sem,
):
    rows = bands_ref.shape[1]
    half = bands_ref.shape[2] // 2
    tiles = half // TILE
    count = half // CHUNK
    kset = lax.axis_index("kset")
    me = lax.axis_index("grid")
    core = lax.rem(me, 2)
    chip = me // 2
    x = lax.rem(chip, 2)
    z = chip // 2

    def device(chip_id, core_id):
        return (kset, chip_id * 2 + core_id)

    mate = device(chip, 1 - core)
    across = device(z * 2 + 1 - x, core)
    parity = lax.rem(z, 2)
    pair = device((z + 1 - 2 * parity) * 2 + x, core)
    cross = device(lax.rem(z + 2, LINE) * 2 + x, core)

    def remote(src, dst, send, recv, target):
        return pltpu.make_async_remote_copy(
            src_ref=src,
            dst_ref=dst,
            send_sem=send,
            recv_sem=recv,
            device_id=target,
            device_id_type=MESH,
        )

    load_b = pltpu.make_async_copy(bands_ref.at[core], mb, load_sem.at[0])
    load_h = pltpu.make_async_copy(hbands_ref.at[core], mh, load_sem.at[1])
    load_b.start()
    load_h.start()
    barrier = pltpu.get_barrier_semaphore()
    pl.semaphore_signal(barrier, inc=1, device_id=mate, device_id_type=MESH)
    for r in range(1, CHIPS):
        pl.semaphore_signal(
            barrier, inc=1, device_id=device(lax.rem(chip + r, CHIPS), core), device_id_type=MESH
        )
    pl.semaphore_wait(barrier, CHIPS)

    swap_b = remote(bands_ref.at[1 - core], rb, in_send.at[0], in_recv.at[0], mate)
    swap_h = remote(hbands_ref.at[1 - core], rh, in_send.at[1], in_recv.at[1], mate)
    swap_b.start()
    swap_h.start()

    def project(band, hband, first, which):
        for i in which:
            lo, hi = i * TILE, (i + 1) * TILE
            a_i = band[:, lo:hi]
            b_i = band[:, half + lo : half + hi]
            ha_i = hband[:, lo:hi]
            hb_i = hband[:, half + lo : half + hi]
            real = (
                dot_t(a_i, hband[:, lo:half])
                + dot_t(b_i, hband[:, half + lo :])
                + dot_t(ha_i, band[:, lo:half])
                + dot_t(hb_i, band[:, half + lo :])
            ) * scale
            imag = (
                dot_t(a_i, hband[:, half : half + hi])
                + dot_t(ha_i, band[:, half : half + hi])
                - dot_t(b_i, hband[:, :hi])
                - dot_t(hb_i, band[:, :hi])
            ) * scale
            r_id = lax.broadcasted_iota(jnp.int32, (TILE, TILE), 0)
            c_id = lax.broadcasted_iota(jnp.int32, (TILE, TILE), 1)
            square_r = real[:, :TILE]
            square_i = imag[:, lo:hi]
            diag = jnp.sum(jnp.where(r_id == c_id, square_r, 0.0), axis=0, keepdims=True)
            mixed = jnp.where(r_id < c_id, square_r, jnp.where(r_id > c_id, square_i, 0.0))
            pieces = [(lo, hi, mixed)]
            if lo > 0:
                pieces.append((0, lo, imag[:, :lo]))
            if hi < half:
                pieces.append((hi, half, real[:, TILE:]))
            for c0, c1, value in pieces:
                if first:
                    packed[lo:hi, c0:c1] = value
                else:
                    packed[lo:hi, c0:c1] = packed[lo:hi, c0:c1] + value
            if first:
                dl[:, lo:hi] = diag
            else:
                dl[:, lo:hi] = dl[:, lo:hi] + diag

    load_b.wait()
    load_h.wait()
    project(mb, mh, True, range(tiles))
    swap_b.wait()
    swap_h.wait()

    copies = {}

    def send(c, stage, src, dst, target):
        copies[c, stage] = remote(src, dst, c_send.at[c, stage], c_recv.at[c, stage], target)
        copies[c, stage].start()

    def places(c):
        half_rows, quarter = CHUNK // 2, CHUNK // 4
        if c % PERIOD == PERIOD - 1:
            first, second, near, far = parity, x, pair, across
        else:
            first, second, near, far = x, parity, across, pair
        mine = c * CHUNK + first * half_rows
        other = c * CHUNK + (1 - first) * half_rows
        own = second * quarter
        rest = (1 - second) * quarter
        return mine, other, own, rest, near, far

    def span(start, size):
        return pl.ds(pl.multiple_of(start, 16), size)

    def begin(c):
        mine, other, own, rest, near, far = places(c)
        s1[c] = packed[span(other, CHUNK // 2), :].astype(jnp.bfloat16)
        send(c, 0, s1.at[c], r1.at[c], near)

    def advance(c, stage):
        mine, other, own, rest, near, far = places(c)
        quarter = CHUNK // 4
        copies[c, stage].wait_recv()
        if stage == 0:
            s2[c] = (
                packed[span(mine + rest, quarter), :]
                + r1[c, span(rest, quarter), :].astype(jnp.float32)
            ).astype(jnp.bfloat16)
            send(c, 1, s2.at[c], r2.at[c], far)
            packed[span(mine + own, quarter), :] = packed[span(mine + own, quarter), :] + r1[
                c, span(own, quarter), :
            ].astype(jnp.float32)
        elif stage == 1:
            value = packed[span(mine + own, quarter), :] + r2[c].astype(jnp.float32)
            s3[c] = value.astype(jnp.bfloat16)
            send(c, 2, s3.at[c], r3.at[c], cross)
            packed[span(mine + own, quarter), :] = value
        elif stage == 2:
            value = packed[span(mine + own, quarter), :] + r3[c].astype(jnp.float32)
            ready = full.at[span(mine + own, quarter), :]
            full[span(mine + own, quarter), :] = value.astype(jnp.bfloat16)
            send(c, 3, ready, ready, far)
            send(c, 4, ready, ready, near)
        elif stage == 3:
            ready = full.at[span(mine + rest, quarter), :]
            send(c, 5, ready, ready, near)

    per_tile = TILE // CHUNK
    for i in range(tiles):
        project(rb, rh, False, (i,))
        for c in range(i * per_tile, (i + 1) * per_tile):
            begin(c)
    traces = []
    for r in range(1, CHIPS):
        copy = remote(
            dl,
            dr.at[r - 1],
            ds_sem.at[r - 1],
            dr_sem.at[r - 1],
            device(lax.rem(chip + r, CHIPS), core),
        )
        copy.start()
        traces.append(copy)
    events = sorted((c + LAG * stage, stage, c) for c in range(count) for stage in range(4))
    for _, stage, c in events:
        advance(c, stage)
    for c in range(count):
        copies[c, 4].wait_recv()
        copies[c, 5].wait_recv()
    diag = dl[...]
    for r in range(1, CHIPS):
        traces[r - 1].wait()
        diag = diag + dr[r - 1]

    level = jnp.sum(diag, axis=1, keepdims=True) / half
    centred = diag - level
    total = jnp.sum(centred * centred, axis=1, keepdims=True)
    square_sum = jnp.zeros((1, half), jnp.float32)
    for i in range(tiles):
        block = full[i * TILE : (i + 1) * TILE, :].astype(jnp.float32)
        square_sum = square_sum + jnp.sum(block * block, axis=0, keepdims=True)
    total = total + 2.0 * jnp.sum(square_sum, axis=1, keepdims=True)
    spread = jnp.sqrt(total / half + 1e-06)
    factor = 1.0 / (4.0 * spread)
    filling = occ_ref[core].astype(jnp.float32) / half
    on_diag = filling - centred * factor
    for i in range(tiles):
        rows_i = slice(i * TILE, (i + 1) * TILE)
        r_id = lax.broadcasted_iota(jnp.int32, (TILE, TILE), 0)
        c_id = lax.broadcasted_iota(jnp.int32, (TILE, TILE), 1)
        block = full[rows_i, rows_i].astype(jnp.float32) * factor
        turned = block.T
        re0[rows_i, rows_i] = jnp.where(
            r_id == c_id, on_diag[:, rows_i], jnp.where(r_id < c_id, -block, -turned)
        ).astype(jnp.bfloat16)
        im0[rows_i, rows_i] = jnp.where(r_id > c_id, -block, turned).astype(jnp.bfloat16)
        for j in range(i + 1, tiles):
            rows_j = slice(j * TILE, (j + 1) * TILE)
            upper = full[rows_i, rows_j].astype(jnp.float32) * factor
            lower = full[rows_j, rows_i].astype(jnp.float32) * factor
            re0[rows_i, rows_j] = (-upper).astype(jnp.bfloat16)
            re0[rows_j, rows_i] = (-upper.T).astype(jnp.bfloat16)
            im0[rows_j, rows_i] = (-lower).astype(jnp.bfloat16)
            im0[rows_i, rows_j] = lower.T.astype(jnp.bfloat16)

    def purify(re, im, re_next, im_next):
        for i in range(tiles):
            lo = i * TILE
            own_rows = slice(lo, lo + TILE)
            right = slice(lo, half)
            r_i, i_i = re[own_rows, :], im[own_rows, :]
            re_c, im_c = re[:, right], im[:, right]
            sq_r = dot(r_i, re_c) - dot(i_i, im_c)
            sq_i = dot(r_i, im_c) + dot(i_i, re_c)
            sr[own_rows, right] = sq_r.astype(jnp.bfloat16)
            si[own_rows, right] = sq_i.astype(jnp.bfloat16)
            for k in range(1, tiles - i):
                part = slice(k * TILE, (k + 1) * TILE)
                below = slice(lo + k * TILE, lo + (k + 1) * TILE)
                sr[below, own_rows] = sq_r[:, part].T.astype(jnp.bfloat16)
                si[below, own_rows] = (-sq_i[:, part].T).astype(jnp.bfloat16)
            s_r, s_i = sr[own_rows, :], si[own_rows, :]
            new_r = 3.0 * sq_r - 2.0 * (dot(s_r, re_c) - dot(s_i, im_c))
            new_i = 3.0 * sq_i - 2.0 * (dot(s_r, im_c) + dot(s_i, re_c))
            re_next[own_rows, right] = new_r.astype(jnp.bfloat16)
            im_next[own_rows, right] = new_i.astype(jnp.bfloat16)
            for k in range(1, tiles - i):
                part = slice(k * TILE, (k + 1) * TILE)
                below = slice(lo + k * TILE, lo + (k + 1) * TILE)
                re_next[below, own_rows] = new_r[:, part].T.astype(jnp.bfloat16)
                im_next[below, own_rows] = (-new_i[:, part].T).astype(jnp.bfloat16)

    bufs = [(re0, im0), (re1, im1)]
    for step in range(MCW):
        purify(*bufs[step % 2], *bufs[(step + 1) % 2])
    re, im = bufs[MCW % 2]

    def update(band, target):
        a, b = band[:, :half], band[:, half:]
        target[:, :half] = (dot(a, re[...]) - dot(b, im[...])).astype(jnp.bfloat16)
        target[:, half:] = (dot(a, im[...]) + dot(b, re[...])).astype(jnp.bfloat16)

    update(rb, ob)
    back = remote(ob, out_ref.at[core], o_sem.at[0], o_sem.at[1], mate)
    back.start()
    update(mb, out_ref.at[core])
    back.wait()
    for copy in copies.values():
        copy.wait_send()


def fused(bands, hbands, occupied):
    points, rows, columns = bands.shape
    half = columns // 2
    count = half // CHUNK
    scale = 1.0 / (2.0 * rows * lax.axis_size("grid"))
    bf16, f32 = jnp.bfloat16, jnp.float32
    dma = pltpu.SemaphoreType.DMA
    return pl.pallas_call(
        functools.partial(kernel, scale),
        out_shape=jax.ShapeDtypeStruct(bands.shape, bf16),
        in_specs=[
            pl.BlockSpec(memory_space=pltpu.SMEM),
            pl.BlockSpec(memory_space=pltpu.HBM),
            pl.BlockSpec(memory_space=pltpu.HBM),
        ],
        out_specs=pl.BlockSpec(memory_space=pltpu.VMEM),
        scratch_shapes=[
            pltpu.VMEM((rows, columns), bf16),
            pltpu.VMEM((rows, columns), bf16),
            pltpu.VMEM((rows, columns), bf16),
            pltpu.VMEM((rows, columns), bf16),
            pltpu.VMEM((half, half), f32),
            pltpu.VMEM((count, CHUNK // 2, half), bf16),
            pltpu.VMEM((count, CHUNK // 2, half), bf16),
            pltpu.VMEM((count, CHUNK // 4, half), bf16),
            pltpu.VMEM((count, CHUNK // 4, half), bf16),
            pltpu.VMEM((count, CHUNK // 4, half), bf16),
            pltpu.VMEM((count, CHUNK // 4, half), bf16),
            pltpu.VMEM((1, half), f32),
            pltpu.VMEM((CHIPS - 1, 1, half), f32),
            pltpu.VMEM((half, half), bf16),
            pltpu.VMEM((half, half), bf16),
            pltpu.VMEM((half, half), bf16),
            pltpu.VMEM((half, half), bf16),
            pltpu.VMEM((half, half), bf16),
            pltpu.VMEM((half, half), bf16),
            pltpu.VMEM((half, half), bf16),
            pltpu.VMEM((rows, columns), bf16),
            dma((2,)),
            dma((2,)),
            dma((CHIPS - 1,)),
            dma((CHIPS - 1,)),
            dma((count, 6)),
            dma((count, 6)),
            dma((2,)),
            dma((2,)),
        ],
        compiler_params=pltpu.CompilerParams(
            collective_id=0, has_side_effects=True, vmem_limit_bytes=61 * 1024 * 1024
        ),
    )(occupied, bands, hbands)


def embedding(full):
    width = full.shape[-1] // 2
    real_part = full[..., :width]
    imag_part = full[..., width:]
    upper = jnp.concatenate([real_part, imag_part], -1)
    lower = jnp.concatenate([-imag_part, real_part], -1)
    return jnp.concatenate([upper, lower], -2)


def spread_out(bands, hbands, occupied):
    points, local_rows, columns = bands.shape
    half = columns // 2
    devices = lax.axis_size("grid")
    share = half // devices
    scale = 1.0 / (2.0 * local_rows * devices)
    blocks = []
    for point in range(points):
        start = jnp.int32(0)
        count = lax.axis_size("grid") * share
        band_k = bands[point]
        hband_k = hbands[point]
        band_cols = jnp.concatenate(
            [
                lax.dynamic_slice_in_dim(band_k, start, count, 1),
                lax.dynamic_slice_in_dim(band_k, half, count, 1),
            ],
            1,
        )
        summed = jnp.einsum("gi,gj->ij", band_cols, hband_k, preferred_element_type=jnp.float32)
        hband_cols = jnp.concatenate(
            [
                lax.dynamic_slice_in_dim(hband_k, start, count, 1),
                lax.dynamic_slice_in_dim(hband_k, half, count, 1),
            ],
            1,
        )
        summed = summed + jnp.einsum(
            "gi,gj->ij", hband_cols, band_k, preferred_element_type=jnp.float32
        )
        real_rows = (summed[:count, :half] + summed[count:, half:]) * scale
        imag_rows = (summed[:count, half:] - summed[count:, :half]) * scale
        blocks.append(
            lax.psum_scatter(
                jnp.concatenate([real_rows, imag_rows], 1), "grid", scatter_dimension=0, tiled=True
            )
        )
    hamiltonian = jnp.stack(blocks, 1)
    hamiltonian = jnp.transpose(hamiltonian, (1, 0, 2))
    ham_real = hamiltonian[:, :, :half]
    ham_imag = hamiltonian[:, :, half:]
    row_index = lax.axis_index("grid") * share + lax.iota(jnp.int32, share)
    col_index = lax.iota(jnp.int32, half)
    identity = (row_index[:, None] == col_index[None, :]).astype(jnp.float32)[None]
    trace_part = jnp.sum(ham_real * identity, axis=(1, 2))
    trace = lax.psum(trace_part, "grid")
    level = (trace / half)[:, None, None]
    centred = ham_real - level * identity
    squares = jnp.sum(centred * centred, axis=(1, 2)) + jnp.sum(ham_imag * ham_imag, axis=(1, 2))
    total = lax.psum(squares, "grid")
    spread = jnp.sqrt(total / half + 1e-06)[:, None, None]
    filling = (occupied.astype(jnp.float32) / half)[:, None, None]
    dens_real = filling * identity - centred / (4.0 * spread)
    dens_imag = -ham_imag / (4.0 * spread)
    density = jnp.concatenate([dens_real, dens_imag], 2).astype(jnp.bfloat16)
    for repeat in range(MCW):
        gathered = lax.all_gather(density, "grid", axis=1, tiled=True)
        matrix = embedding(gathered)
        square = jnp.einsum("krc,kcd->krd", density, matrix, preferred_element_type=jnp.float32)
        cube = jnp.einsum(
            "krc,kcd->krd", square.astype(jnp.bfloat16), matrix, preferred_element_type=jnp.float32
        )
        density = (3.0 * square - 2.0 * cube).astype(jnp.bfloat16)
    gathered = lax.all_gather(density, "grid", axis=1, tiled=True)
    matrix = embedding(gathered)
    updated = jnp.einsum("kgc,kcd->kgd", bands, matrix, preferred_element_type=jnp.float32)
    return updated.astype(jnp.bfloat16)


def on_device(bands, hbands, occupied):
    points, rows, columns = bands.shape
    half = columns // 2
    if (
        lax.axis_size("grid") == 2 * CHIPS
        and points == 2
        and half % TILE == 0
        and half % (16 * CHIPS) == 0
    ):
        return fused(bands, hbands, occupied)
    return spread_out(bands, hbands, occupied)


def solution(mesh):
    return jax.shard_map(
        on_device,
        mesh=mesh,
        in_specs=(P("kset", "grid", None), P("kset", "grid", None), P("kset")),
        out_specs=P("kset", "grid", None),
        check_vma=False,
    )
```

```python
import functools

import jax
import jax.numpy as jnp
from jax import lax
from jax.experimental import pallas as pl
from jax.experimental.pallas import tpu as pltpu
from jax.sharding import PartitionSpec as P

MCW = 2
LINE = 4
CHIPS = 2 * LINE
TILE = 256
CHUNK = 128
PERIOD = 3
LAG = 2
MESH = pl.DeviceIdType.MESH


def dot_t(left, right):
    return lax.dot_general(
        left, right, (((0,), (0,)), ((), ())), preferred_element_type=jnp.float32
    )


def dot(left, right):
    return jnp.dot(left, right, preferred_element_type=jnp.float32)


def kernel(
    scale,
    occ_ref,
    bands_ref,
    hbands_ref,
    out_ref,
    mb,
    mh,
    rb,
    rh,
    packed,
    s1,
    r1,
    s2,
    r2,
    s3,
    r3,
    dl,
    dr,
    full,
    re0,
    im0,
    m0,
    re1,
    im1,
    m1,
    sr,
    si,
    sum_m,
    sum_r,
    ob,
    in_send,
    in_recv,
    ds_sem,
    dr_sem,
    c_send,
    c_recv,
    o_sem,
    load_sem,
):
    rows = bands_ref.shape[1]
    half = bands_ref.shape[2] // 2
    tiles = half // TILE
    count = half // CHUNK
    kset = lax.axis_index("kset")
    me = lax.axis_index("grid")
    core = lax.rem(me, 2)
    chip = me // 2
    x = lax.rem(chip, 2)
    z = chip // 2

    def device(chip_id, core_id):
        return (kset, chip_id * 2 + core_id)

    mate = device(chip, 1 - core)
    across = device(z * 2 + 1 - x, core)
    parity = lax.rem(z, 2)
    pair = device((z + 1 - 2 * parity) * 2 + x, core)
    cross = device(lax.rem(z + 2, LINE) * 2 + x, core)

    def remote(src, dst, send, recv, target):
        return pltpu.make_async_remote_copy(
            src_ref=src,
            dst_ref=dst,
            send_sem=send,
            recv_sem=recv,
            device_id=target,
            device_id_type=MESH,
        )

    load_b = pltpu.make_async_copy(bands_ref.at[core], mb, load_sem.at[0])
    load_h = pltpu.make_async_copy(hbands_ref.at[core], mh, load_sem.at[1])
    load_b.start()
    load_h.start()
    barrier = pltpu.get_barrier_semaphore()
    pl.semaphore_signal(barrier, inc=1, device_id=mate, device_id_type=MESH)
    for r in range(1, CHIPS):
        pl.semaphore_signal(
            barrier, inc=1, device_id=device(lax.rem(chip + r, CHIPS), core), device_id_type=MESH
        )
    pl.semaphore_wait(barrier, CHIPS)

    swap_b = remote(bands_ref.at[1 - core], rb, in_send.at[0], in_recv.at[0], mate)
    swap_h = remote(hbands_ref.at[1 - core], rh, in_send.at[1], in_recv.at[1], mate)
    swap_b.start()
    swap_h.start()

    def project(band, hband, first, which):
        for i in which:
            lo, hi = i * TILE, (i + 1) * TILE
            a_i = band[:, lo:hi]
            b_i = band[:, half + lo : half + hi]
            ha_i = hband[:, lo:hi]
            hb_i = hband[:, half + lo : half + hi]
            real = (
                dot_t(a_i, hband[:, lo:half])
                + dot_t(b_i, hband[:, half + lo :])
                + dot_t(ha_i, band[:, lo:half])
                + dot_t(hb_i, band[:, half + lo :])
            ) * scale
            imag = (
                dot_t(a_i, hband[:, half : half + hi])
                + dot_t(ha_i, band[:, half : half + hi])
                - dot_t(b_i, hband[:, :hi])
                - dot_t(hb_i, band[:, :hi])
            ) * scale
            r_id = lax.broadcasted_iota(jnp.int32, (TILE, TILE), 0)
            c_id = lax.broadcasted_iota(jnp.int32, (TILE, TILE), 1)
            square_r = real[:, :TILE]
            square_i = imag[:, lo:hi]
            diag = jnp.sum(jnp.where(r_id == c_id, square_r, 0.0), axis=0, keepdims=True)
            mixed = jnp.where(r_id < c_id, square_r, jnp.where(r_id > c_id, square_i, 0.0))
            pieces = [(lo, hi, mixed)]
            if lo > 0:
                pieces.append((0, lo, imag[:, :lo]))
            if hi < half:
                pieces.append((hi, half, real[:, TILE:]))
            for c0, c1, value in pieces:
                if first:
                    packed[lo:hi, c0:c1] = value
                else:
                    packed[lo:hi, c0:c1] = packed[lo:hi, c0:c1] + value
            if first:
                dl[:, lo:hi] = diag
            else:
                dl[:, lo:hi] = dl[:, lo:hi] + diag

    load_b.wait()
    load_h.wait()
    project(mb, mh, True, range(tiles))
    swap_b.wait()
    swap_h.wait()

    copies = {}

    def send(c, stage, src, dst, target):
        copies[c, stage] = remote(src, dst, c_send.at[c, stage], c_recv.at[c, stage], target)
        copies[c, stage].start()

    def places(c):
        half_rows, quarter = CHUNK // 2, CHUNK // 4
        if c % PERIOD == PERIOD - 1:
            first, second, near, far = parity, x, pair, across
        else:
            first, second, near, far = x, parity, across, pair
        mine = c * CHUNK + first * half_rows
        other = c * CHUNK + (1 - first) * half_rows
        own = second * quarter
        rest = (1 - second) * quarter
        return mine, other, own, rest, near, far

    def span(start, size):
        return pl.ds(pl.multiple_of(start, 16), size)

    def begin(c):
        mine, other, own, rest, near, far = places(c)
        s1[c] = packed[span(other, CHUNK // 2), :].astype(jnp.bfloat16)
        send(c, 0, s1.at[c], r1.at[c], near)

    def advance(c, stage):
        mine, other, own, rest, near, far = places(c)
        quarter = CHUNK // 4
        copies[c, stage].wait_recv()
        if stage == 0:
            s2[c] = (
                packed[span(mine + rest, quarter), :]
                + r1[c, span(rest, quarter), :].astype(jnp.float32)
            ).astype(jnp.bfloat16)
            send(c, 1, s2.at[c], r2.at[c], far)
            packed[span(mine + own, quarter), :] = packed[span(mine + own, quarter), :] + r1[
                c, span(own, quarter), :
            ].astype(jnp.float32)
        elif stage == 1:
            value = packed[span(mine + own, quarter), :] + r2[c].astype(jnp.float32)
            s3[c] = value.astype(jnp.bfloat16)
            send(c, 2, s3.at[c], r3.at[c], cross)
            packed[span(mine + own, quarter), :] = value
        elif stage == 2:
            value = packed[span(mine + own, quarter), :] + r3[c].astype(jnp.float32)
            ready = full.at[span(mine + own, quarter), :]
            full[span(mine + own, quarter), :] = value.astype(jnp.bfloat16)
            send(c, 3, ready, ready, far)
            send(c, 4, ready, ready, near)
        elif stage == 3:
            ready = full.at[span(mine + rest, quarter), :]
            send(c, 5, ready, ready, near)

    per_tile = TILE // CHUNK
    for i in range(tiles):
        project(rb, rh, False, (i,))
        for c in range(i * per_tile, (i + 1) * per_tile):
            begin(c)
    traces = []
    for r in range(1, CHIPS):
        copy = remote(
            dl,
            dr.at[r - 1],
            ds_sem.at[r - 1],
            dr_sem.at[r - 1],
            device(lax.rem(chip + r, CHIPS), core),
        )
        copy.start()
        traces.append(copy)
    for band, band_sum in ((mb, sum_m), (rb, sum_r)):
        band_sum[...] = band[:, :half] + band[:, half:]
    events = sorted((c + LAG * stage, stage, c) for c in range(count) for stage in range(4))
    for _, stage, c in events:
        advance(c, stage)
    for c in range(count):
        copies[c, 4].wait_recv()
        copies[c, 5].wait_recv()
    diag = dl[...]
    for r in range(1, CHIPS):
        traces[r - 1].wait()
        diag = diag + dr[r - 1]

    level = jnp.sum(diag, axis=1, keepdims=True) / half
    centred = diag - level
    total = jnp.sum(centred * centred, axis=1, keepdims=True)
    square_sum = jnp.zeros((1, half), jnp.float32)
    for i in range(tiles):
        block = full[i * TILE : (i + 1) * TILE, :].astype(jnp.float32)
        square_sum = square_sum + jnp.sum(block * block, axis=0, keepdims=True)
    total = total + 2.0 * jnp.sum(square_sum, axis=1, keepdims=True)
    spread = jnp.sqrt(total / half + 1e-06)
    factor = 1.0 / (4.0 * spread)
    filling = occ_ref[core].astype(jnp.float32) / half
    on_diag = filling - centred * factor
    for i in range(tiles):
        rows_i = slice(i * TILE, (i + 1) * TILE)
        r_id = lax.broadcasted_iota(jnp.int32, (TILE, TILE), 0)
        c_id = lax.broadcasted_iota(jnp.int32, (TILE, TILE), 1)
        block = full[rows_i, rows_i].astype(jnp.float32) * factor
        turned = block.T
        re0[rows_i, rows_i] = jnp.where(
            r_id == c_id, on_diag[:, rows_i], jnp.where(r_id < c_id, -block, -turned)
        ).astype(jnp.bfloat16)
        im0[rows_i, rows_i] = jnp.where(r_id > c_id, -block, turned).astype(jnp.bfloat16)
        for j in range(i + 1, tiles):
            rows_j = slice(j * TILE, (j + 1) * TILE)
            upper = full[rows_i, rows_j].astype(jnp.float32) * factor
            lower = full[rows_j, rows_i].astype(jnp.float32) * factor
            re0[rows_i, rows_j] = (-upper).astype(jnp.bfloat16)
            re0[rows_j, rows_i] = (-upper.T).astype(jnp.bfloat16)
            im0[rows_j, rows_i] = (-lower).astype(jnp.bfloat16)
            im0[rows_i, rows_j] = lower.T.astype(jnp.bfloat16)

    def three(left, right):
        p = dot(left[0], right[0])
        q = dot(left[1], right[1])
        return p - q, dot(left[2], right[2]) - (p + q)

    def mirror(i, refs, real, imag):
        lo = i * TILE
        real, imag = real.astype(jnp.bfloat16), imag.astype(jnp.bfloat16)
        own_rows, right = slice(lo, lo + TILE), slice(lo, half)
        places = [(own_rows, right, real, imag)]
        for k in range(1, tiles - i):
            part = slice(k * TILE, (k + 1) * TILE)
            below = slice(lo + k * TILE, lo + (k + 1) * TILE)
            places.append((below, own_rows, real[:, part].T, -imag[:, part].T))
        for down, along, r, i in places:
            for ref, value in zip(refs, (r, i, r + i)):
                ref[down, along] = value

    def purify(now, following):
        for i in range(tiles):
            lo = i * TILE
            own_rows = slice(lo, lo + TILE)
            right = slice(lo, half)
            columns = [ref[:, right] for ref in now]
            sq_r, sq_i = three([ref[own_rows, :] for ref in now], columns)
            mirror(i, (sr, si), sq_r, sq_i)
            s_r, s_i = sr[own_rows, :], si[own_rows, :]
            cube_r, cube_i = three([s_r, s_i, s_r + s_i], columns)
            mirror(i, following, 3.0 * sq_r - 2.0 * cube_r, 3.0 * sq_i - 2.0 * cube_i)

    m0[...] = re0[...] + im0[...]
    bufs = [(re0, im0, m0), (re1, im1, m1)]
    for step in range(MCW):
        purify(bufs[step % 2], bufs[(step + 1) % 2])
    last = [ref[...] for ref in bufs[MCW % 2]]

    def update(band, band_sum, target):
        real, imag = three([band[:, :half], band[:, half:], band_sum[...]], last)
        target[:, :half] = real.astype(jnp.bfloat16)
        target[:, half:] = imag.astype(jnp.bfloat16)

    update(rb, sum_r, ob)
    back = remote(ob, out_ref.at[core], o_sem.at[0], o_sem.at[1], mate)
    back.start()
    update(mb, sum_m, out_ref.at[core])
    back.wait()
    for copy in copies.values():
        copy.wait_send()


def fused(bands, hbands, occupied):
    points, rows, columns = bands.shape
    half = columns // 2
    count = half // CHUNK
    scale = 1.0 / (2.0 * rows * lax.axis_size("grid"))
    bf16, f32 = jnp.bfloat16, jnp.float32
    dma = pltpu.SemaphoreType.DMA
    return pl.pallas_call(
        functools.partial(kernel, scale),
        out_shape=jax.ShapeDtypeStruct(bands.shape, bf16),
        in_specs=[
            pl.BlockSpec(memory_space=pltpu.SMEM),
            pl.BlockSpec(memory_space=pltpu.HBM),
            pl.BlockSpec(memory_space=pltpu.HBM),
        ],
        out_specs=pl.BlockSpec(memory_space=pltpu.VMEM),
        scratch_shapes=[
            pltpu.VMEM((rows, columns), bf16),
            pltpu.VMEM((rows, columns), bf16),
            pltpu.VMEM((rows, columns), bf16),
            pltpu.VMEM((rows, columns), bf16),
            pltpu.VMEM((half, half), f32),
            pltpu.VMEM((count, CHUNK // 2, half), bf16),
            pltpu.VMEM((count, CHUNK // 2, half), bf16),
            pltpu.VMEM((count, CHUNK // 4, half), bf16),
            pltpu.VMEM((count, CHUNK // 4, half), bf16),
            pltpu.VMEM((count, CHUNK // 4, half), bf16),
            pltpu.VMEM((count, CHUNK // 4, half), bf16),
            pltpu.VMEM((1, half), f32),
            pltpu.VMEM((CHIPS - 1, 1, half), f32),
            pltpu.VMEM((half, half), bf16),
            pltpu.VMEM((half, half), bf16),
            pltpu.VMEM((half, half), bf16),
            pltpu.VMEM((half, half), bf16),
            pltpu.VMEM((half, half), bf16),
            pltpu.VMEM((half, half), bf16),
            pltpu.VMEM((half, half), bf16),
            pltpu.VMEM((half, half), bf16),
            pltpu.VMEM((half, half), bf16),
            pltpu.VMEM((rows, half), bf16),
            pltpu.VMEM((rows, half), bf16),
            pltpu.VMEM((rows, columns), bf16),
            dma((2,)),
            dma((2,)),
            dma((CHIPS - 1,)),
            dma((CHIPS - 1,)),
            dma((count, 6)),
            dma((count, 6)),
            dma((2,)),
            dma((2,)),
        ],
        compiler_params=pltpu.CompilerParams(
            collective_id=0, has_side_effects=True, vmem_limit_bytes=61 * 1024 * 1024
        ),
    )(occupied, bands, hbands)


def embedding(full):
    width = full.shape[-1] // 2
    real_part = full[..., :width]
    imag_part = full[..., width:]
    upper = jnp.concatenate([real_part, imag_part], -1)
    lower = jnp.concatenate([-imag_part, real_part], -1)
    return jnp.concatenate([upper, lower], -2)


def spread_out(bands, hbands, occupied):
    points, local_rows, columns = bands.shape
    half = columns // 2
    devices = lax.axis_size("grid")
    share = half // devices
    scale = 1.0 / (2.0 * local_rows * devices)
    blocks = []
    for point in range(points):
        start = jnp.int32(0)
        count = lax.axis_size("grid") * share
        band_k = bands[point]
        hband_k = hbands[point]
        band_cols = jnp.concatenate(
            [
                lax.dynamic_slice_in_dim(band_k, start, count, 1),
                lax.dynamic_slice_in_dim(band_k, half, count, 1),
            ],
            1,
        )
        summed = jnp.einsum("gi,gj->ij", band_cols, hband_k, preferred_element_type=jnp.float32)
        hband_cols = jnp.concatenate(
            [
                lax.dynamic_slice_in_dim(hband_k, start, count, 1),
                lax.dynamic_slice_in_dim(hband_k, half, count, 1),
            ],
            1,
        )
        summed = summed + jnp.einsum(
            "gi,gj->ij", hband_cols, band_k, preferred_element_type=jnp.float32
        )
        real_rows = (summed[:count, :half] + summed[count:, half:]) * scale
        imag_rows = (summed[:count, half:] - summed[count:, :half]) * scale
        blocks.append(
            lax.psum_scatter(
                jnp.concatenate([real_rows, imag_rows], 1), "grid", scatter_dimension=0, tiled=True
            )
        )
    hamiltonian = jnp.stack(blocks, 1)
    hamiltonian = jnp.transpose(hamiltonian, (1, 0, 2))
    ham_real = hamiltonian[:, :, :half]
    ham_imag = hamiltonian[:, :, half:]
    row_index = lax.axis_index("grid") * share + lax.iota(jnp.int32, share)
    col_index = lax.iota(jnp.int32, half)
    identity = (row_index[:, None] == col_index[None, :]).astype(jnp.float32)[None]
    trace_part = jnp.sum(ham_real * identity, axis=(1, 2))
    trace = lax.psum(trace_part, "grid")
    level = (trace / half)[:, None, None]
    centred = ham_real - level * identity
    squares = jnp.sum(centred * centred, axis=(1, 2)) + jnp.sum(ham_imag * ham_imag, axis=(1, 2))
    total = lax.psum(squares, "grid")
    spread = jnp.sqrt(total / half + 1e-06)[:, None, None]
    filling = (occupied.astype(jnp.float32) / half)[:, None, None]
    dens_real = filling * identity - centred / (4.0 * spread)
    dens_imag = -ham_imag / (4.0 * spread)
    density = jnp.concatenate([dens_real, dens_imag], 2).astype(jnp.bfloat16)
    for repeat in range(MCW):
        gathered = lax.all_gather(density, "grid", axis=1, tiled=True)
        matrix = embedding(gathered)
        square = jnp.einsum("krc,kcd->krd", density, matrix, preferred_element_type=jnp.float32)
        cube = jnp.einsum(
            "krc,kcd->krd", square.astype(jnp.bfloat16), matrix, preferred_element_type=jnp.float32
        )
        density = (3.0 * square - 2.0 * cube).astype(jnp.bfloat16)
    gathered = lax.all_gather(density, "grid", axis=1, tiled=True)
    matrix = embedding(gathered)
    updated = jnp.einsum("kgc,kcd->kgd", bands, matrix, preferred_element_type=jnp.float32)
    return updated.astype(jnp.bfloat16)


def on_device(bands, hbands, occupied):
    points, rows, columns = bands.shape
    half = columns // 2
    if (
        lax.axis_size("grid") == 2 * CHIPS
        and points == 2
        and half % TILE == 0
        and half % (16 * CHIPS) == 0
    ):
        return fused(bands, hbands, occupied)
    return spread_out(bands, hbands, occupied)


def solution(mesh):
    return jax.shard_map(
        on_device,
        mesh=mesh,
        in_specs=(P("kset", "grid", None), P("kset", "grid", None), P("kset")),
        out_specs=P("kset", "grid", None),
        check_vma=False,
    )
```

```python
import functools

import jax
import jax.numpy as jnp
from jax import lax
from jax.experimental import pallas as pl
from jax.experimental.pallas import tpu as pltpu
from jax.sharding import PartitionSpec as P

MCW = 2
LINE = 4
CHIPS = 2 * LINE
TILE = 256
CHUNK = 128
PERIOD = 3
LAG = 2
MESH = pl.DeviceIdType.MESH


def dot_t(left, right):
    return lax.dot_general(
        left, right, (((0,), (0,)), ((), ())), preferred_element_type=jnp.float32
    )


def dot(left, right):
    return jnp.dot(left, right, preferred_element_type=jnp.float32)


def kernel(
    scale,
    occ_ref,
    bands_ref,
    hbands_ref,
    out_ref,
    mb,
    mh,
    rb,
    rh,
    packed,
    s1,
    r1,
    s2,
    r2,
    s3,
    r3,
    dl,
    dr,
    full,
    re0,
    im0,
    m0,
    re1,
    im1,
    m1,
    sr,
    si,
    sum_m,
    sum_r,
    ob,
    in_send,
    in_recv,
    ds_sem,
    dr_sem,
    c_send,
    c_recv,
    o_sem,
    load_sem,
):
    rows = bands_ref.shape[1]
    half = bands_ref.shape[2] // 2
    tiles = half // TILE
    count = half // CHUNK
    kset = lax.axis_index("kset")
    me = lax.axis_index("grid")
    core = lax.rem(me, 2)
    chip = me // 2
    x = lax.rem(chip, 2)
    z = chip // 2

    def device(chip_id, core_id):
        return (kset, chip_id * 2 + core_id)

    mate = device(chip, 1 - core)
    across = device(z * 2 + 1 - x, core)
    parity = lax.rem(z, 2)
    pair = device((z + 1 - 2 * parity) * 2 + x, core)
    cross = device(lax.rem(z + 2, LINE) * 2 + x, core)

    def remote(src, dst, send, recv, target):
        return pltpu.make_async_remote_copy(
            src_ref=src,
            dst_ref=dst,
            send_sem=send,
            recv_sem=recv,
            device_id=target,
            device_id_type=MESH,
        )

    load_b = pltpu.make_async_copy(bands_ref.at[core], mb, load_sem.at[0])
    load_h = pltpu.make_async_copy(hbands_ref.at[core], mh, load_sem.at[1])
    load_b.start()
    load_h.start()
    barrier = pltpu.get_barrier_semaphore()
    pl.semaphore_signal(barrier, inc=1, device_id=mate, device_id_type=MESH)
    for r in range(1, CHIPS):
        pl.semaphore_signal(
            barrier, inc=1, device_id=device(lax.rem(chip + r, CHIPS), core), device_id_type=MESH
        )
    pl.semaphore_wait(barrier, CHIPS)

    swap_b = remote(bands_ref.at[1 - core], rb, in_send.at[0], in_recv.at[0], mate)
    swap_h = remote(hbands_ref.at[1 - core], rh, in_send.at[1], in_recv.at[1], mate)
    swap_b.start()
    swap_h.start()

    def project(band, hband, first, which):
        for i in which:
            lo, hi = i * TILE, (i + 1) * TILE
            a_i = band[:, lo:hi]
            b_i = band[:, half + lo : half + hi]
            ha_i = hband[:, lo:hi]
            hb_i = hband[:, half + lo : half + hi]
            real = (
                dot_t(a_i, hband[:, lo:half])
                + dot_t(b_i, hband[:, half + lo :])
                + dot_t(ha_i, band[:, lo:half])
                + dot_t(hb_i, band[:, half + lo :])
            ) * scale
            imag = (
                dot_t(a_i, hband[:, half : half + hi])
                + dot_t(ha_i, band[:, half : half + hi])
                - dot_t(b_i, hband[:, :hi])
                - dot_t(hb_i, band[:, :hi])
            ) * scale
            r_id = lax.broadcasted_iota(jnp.int32, (TILE, TILE), 0)
            c_id = lax.broadcasted_iota(jnp.int32, (TILE, TILE), 1)
            square_r = real[:, :TILE]
            square_i = imag[:, lo:hi]
            diag = jnp.sum(jnp.where(r_id == c_id, square_r, 0.0), axis=0, keepdims=True)
            mixed = jnp.where(r_id < c_id, square_r, jnp.where(r_id > c_id, square_i, 0.0))
            pieces = [(lo, hi, mixed)]
            if lo > 0:
                pieces.append((0, lo, imag[:, :lo]))
            if hi < half:
                pieces.append((hi, half, real[:, TILE:]))
            for c0, c1, value in pieces:
                if first:
                    packed[lo:hi, c0:c1] = value
                else:
                    packed[lo:hi, c0:c1] = packed[lo:hi, c0:c1] + value
            if first:
                dl[:, lo:hi] = diag
            else:
                dl[:, lo:hi] = dl[:, lo:hi] + diag

    load_b.wait()
    load_h.wait()
    project(mb, mh, True, range(tiles))
    swap_b.wait()
    swap_h.wait()

    copies = {}

    def send(c, stage, src, dst, target):
        copies[c, stage] = remote(src, dst, c_send.at[c, stage], c_recv.at[c, stage], target)
        copies[c, stage].start()

    def places(c):
        half_rows, quarter = CHUNK // 2, CHUNK // 4
        if c % PERIOD == PERIOD - 1:
            first, second, near, far = parity, x, pair, across
        else:
            first, second, near, far = x, parity, across, pair
        mine = c * CHUNK + first * half_rows
        other = c * CHUNK + (1 - first) * half_rows
        own = second * quarter
        rest = (1 - second) * quarter
        return mine, other, own, rest, near, far

    def span(start, size):
        return pl.ds(pl.multiple_of(start, 16), size)

    def begin(c):
        mine, other, own, rest, near, far = places(c)
        s1[c] = packed[span(other, CHUNK // 2), :].astype(jnp.bfloat16)
        send(c, 0, s1.at[c], r1.at[c], near)

    def advance(c, stage):
        mine, other, own, rest, near, far = places(c)
        quarter = CHUNK // 4
        copies[c, stage].wait_recv()
        if stage == 0:
            s2[c] = (
                packed[span(mine + rest, quarter), :]
                + r1[c, span(rest, quarter), :].astype(jnp.float32)
            ).astype(jnp.bfloat16)
            send(c, 1, s2.at[c], r2.at[c], far)
            packed[span(mine + own, quarter), :] = packed[span(mine + own, quarter), :] + r1[
                c, span(own, quarter), :
            ].astype(jnp.float32)
        elif stage == 1:
            value = packed[span(mine + own, quarter), :] + r2[c].astype(jnp.float32)
            s3[c] = value.astype(jnp.bfloat16)
            send(c, 2, s3.at[c], r3.at[c], cross)
            packed[span(mine + own, quarter), :] = value
        elif stage == 2:
            value = packed[span(mine + own, quarter), :] + r3[c].astype(jnp.float32)
            ready = full.at[span(mine + own, quarter), :]
            full[span(mine + own, quarter), :] = value.astype(jnp.bfloat16)
            send(c, 3, ready, ready, far)
            send(c, 4, ready, ready, near)
        elif stage == 3:
            ready = full.at[span(mine + rest, quarter), :]
            send(c, 5, ready, ready, near)

    per_tile = TILE // CHUNK
    for i in range(tiles):
        project(rb, rh, False, (i,))
        for c in range(i * per_tile, (i + 1) * per_tile):
            begin(c)
    traces = []
    for r in range(1, CHIPS):
        copy = remote(
            dl,
            dr.at[r - 1],
            ds_sem.at[r - 1],
            dr_sem.at[r - 1],
            device(lax.rem(chip + r, CHIPS), core),
        )
        copy.start()
        traces.append(copy)
    for band, band_sum in ((mb, sum_m), (rb, sum_r)):
        band_sum[...] = band[:, :half] + band[:, half:]
    events = sorted((c + LAG * stage, stage, c) for c in range(count) for stage in range(4))
    for _, stage, c in events:
        advance(c, stage)
    for c in range(count):
        copies[c, 4].wait_recv()
        copies[c, 5].wait_recv()
    diag = dl[...]
    for r in range(1, CHIPS):
        traces[r - 1].wait()
        diag = diag + dr[r - 1]

    level = jnp.sum(diag, axis=1, keepdims=True) / half
    centred = diag - level
    total = jnp.sum(centred * centred, axis=1, keepdims=True)
    square_sum = jnp.zeros((1, half), jnp.float32)
    for i in range(tiles):
        block = full[i * TILE : (i + 1) * TILE, :].astype(jnp.float32)
        square_sum = square_sum + jnp.sum(block * block, axis=0, keepdims=True)
    total = total + 2.0 * jnp.sum(square_sum, axis=1, keepdims=True)
    spread = jnp.sqrt(total / half + 1e-06)
    factor = 1.0 / (4.0 * spread)
    filling = occ_ref[core].astype(jnp.float32) / half
    on_diag = filling - centred * factor
    for i in range(tiles):
        rows_i = slice(i * TILE, (i + 1) * TILE)
        r_id = lax.broadcasted_iota(jnp.int32, (TILE, TILE), 0)
        c_id = lax.broadcasted_iota(jnp.int32, (TILE, TILE), 1)
        block = full[rows_i, rows_i].astype(jnp.float32) * factor
        turned = block.T
        re0[rows_i, rows_i] = jnp.where(
            r_id == c_id, on_diag[:, rows_i], jnp.where(r_id < c_id, -block, -turned)
        ).astype(jnp.bfloat16)
        im0[rows_i, rows_i] = jnp.where(r_id > c_id, -block, turned).astype(jnp.bfloat16)
        for j in range(i + 1, tiles):
            rows_j = slice(j * TILE, (j + 1) * TILE)
            upper = full[rows_i, rows_j].astype(jnp.float32) * factor
            lower = full[rows_j, rows_i].astype(jnp.float32) * factor
            re0[rows_i, rows_j] = (-upper).astype(jnp.bfloat16)
            re0[rows_j, rows_i] = (-upper.T).astype(jnp.bfloat16)
            im0[rows_j, rows_i] = (-lower).astype(jnp.bfloat16)
            im0[rows_i, rows_j] = lower.T.astype(jnp.bfloat16)

    def three(left, right):
        p = dot(left[0], right[0])
        q = dot(left[1], right[1])
        return p - q, dot(left[2], right[2]) - (p + q)

    def mirror(i, refs, real, imag):
        lo = i * TILE
        real, imag = real.astype(jnp.bfloat16), imag.astype(jnp.bfloat16)
        own_rows, right = slice(lo, lo + TILE), slice(lo, half)
        places = [(own_rows, right, real, imag)]
        for k in range(1, tiles - i):
            part = slice(k * TILE, (k + 1) * TILE)
            below = slice(lo + k * TILE, lo + (k + 1) * TILE)
            places.append((below, own_rows, real[:, part].T, -imag[:, part].T))
        for down, along, r, i in places:
            for ref, value in zip(refs, (r, i, r + i)):
                ref[down, along] = value

    def purify(now, following):
        for i in range(tiles):
            lo = i * TILE
            own_rows = slice(lo, lo + TILE)
            right = slice(lo, half)
            columns = [ref[:, right] for ref in now]
            sq_r, sq_i = three([ref[own_rows, :] for ref in now], columns)
            mirror(i, (sr, si), sq_r, sq_i)
            s_r, s_i = sr[own_rows, :], si[own_rows, :]
            cube_r, cube_i = three([s_r, s_i, s_r + s_i], columns)
            mirror(i, following, 3.0 * sq_r - 2.0 * cube_r, 3.0 * sq_i - 2.0 * cube_i)

    m0[...] = re0[...] + im0[...]
    bufs = [(re0, im0, m0), (re1, im1, m1)]
    for step in range(MCW):
        purify(bufs[step % 2], bufs[(step + 1) % 2])
    last = [ref[...] for ref in bufs[MCW % 2]]

    def update(band, band_sum, target):
        real, imag = three([band[:, :half], band[:, half:], band_sum[...]], last)
        target[:, :half] = real.astype(jnp.bfloat16)
        target[:, half:] = imag.astype(jnp.bfloat16)

    update(rb, sum_r, ob)
    back = remote(ob, out_ref.at[core], o_sem.at[0], o_sem.at[1], mate)
    back.start()
    update(mb, sum_m, out_ref.at[core])
    back.wait()
    for copy in copies.values():
        copy.wait_send()


def fused(bands, hbands, occupied):
    points, rows, columns = bands.shape
    half = columns // 2
    count = half // CHUNK
    scale = 1.0 / (2.0 * rows * lax.axis_size("grid"))
    bf16, f32 = jnp.bfloat16, jnp.float32
    dma = pltpu.SemaphoreType.DMA
    return pl.pallas_call(
        functools.partial(kernel, scale),
        out_shape=pltpu.VMEM(bands.shape, bf16),
        in_specs=[
            pl.BlockSpec(memory_space=pltpu.SMEM),
            pl.BlockSpec(memory_space=pltpu.HBM),
            pl.BlockSpec(memory_space=pltpu.HBM),
        ],
        out_specs=pl.BlockSpec(memory_space=pltpu.VMEM),
        scratch_shapes=[
            pltpu.VMEM((rows, columns), bf16),
            pltpu.VMEM((rows, columns), bf16),
            pltpu.VMEM((rows, columns), bf16),
            pltpu.VMEM((rows, columns), bf16),
            pltpu.VMEM((half, half), f32),
            pltpu.VMEM((count, CHUNK // 2, half), bf16),
            pltpu.VMEM((count, CHUNK // 2, half), bf16),
            pltpu.VMEM((count, CHUNK // 4, half), bf16),
            pltpu.VMEM((count, CHUNK // 4, half), bf16),
            pltpu.VMEM((count, CHUNK // 4, half), bf16),
            pltpu.VMEM((count, CHUNK // 4, half), bf16),
            pltpu.VMEM((1, half), f32),
            pltpu.VMEM((CHIPS - 1, 1, half), f32),
            pltpu.VMEM((half, half), bf16),
            pltpu.VMEM((half, half), bf16),
            pltpu.VMEM((half, half), bf16),
            pltpu.VMEM((half, half), bf16),
            pltpu.VMEM((half, half), bf16),
            pltpu.VMEM((half, half), bf16),
            pltpu.VMEM((half, half), bf16),
            pltpu.VMEM((half, half), bf16),
            pltpu.VMEM((half, half), bf16),
            pltpu.VMEM((rows, half), bf16),
            pltpu.VMEM((rows, half), bf16),
            pltpu.VMEM((rows, columns), bf16),
            dma((2,)),
            dma((2,)),
            dma((CHIPS - 1,)),
            dma((CHIPS - 1,)),
            dma((count, 6)),
            dma((count, 6)),
            dma((2,)),
            dma((2,)),
        ],
        compiler_params=pltpu.CompilerParams(
            collective_id=0, has_side_effects=True, vmem_limit_bytes=40 * 1024 * 1024
        ),
    )(*(pltpu.with_memory_space_constraint(x, pltpu.HBM) for x in (occupied, bands, hbands)))


def embedding(full):
    width = full.shape[-1] // 2
    real_part = full[..., :width]
    imag_part = full[..., width:]
    upper = jnp.concatenate([real_part, imag_part], -1)
    lower = jnp.concatenate([-imag_part, real_part], -1)
    return jnp.concatenate([upper, lower], -2)


def spread_out(bands, hbands, occupied):
    points, local_rows, columns = bands.shape
    half = columns // 2
    devices = lax.axis_size("grid")
    share = half // devices
    scale = 1.0 / (2.0 * local_rows * devices)
    blocks = []
    for point in range(points):
        start = jnp.int32(0)
        count = lax.axis_size("grid") * share
        band_k = bands[point]
        hband_k = hbands[point]
        band_cols = jnp.concatenate(
            [
                lax.dynamic_slice_in_dim(band_k, start, count, 1),
                lax.dynamic_slice_in_dim(band_k, half, count, 1),
            ],
            1,
        )
        summed = jnp.einsum("gi,gj->ij", band_cols, hband_k, preferred_element_type=jnp.float32)
        hband_cols = jnp.concatenate(
            [
                lax.dynamic_slice_in_dim(hband_k, start, count, 1),
                lax.dynamic_slice_in_dim(hband_k, half, count, 1),
            ],
            1,
        )
        summed = summed + jnp.einsum(
            "gi,gj->ij", hband_cols, band_k, preferred_element_type=jnp.float32
        )
        real_rows = (summed[:count, :half] + summed[count:, half:]) * scale
        imag_rows = (summed[:count, half:] - summed[count:, :half]) * scale
        blocks.append(
            lax.psum_scatter(
                jnp.concatenate([real_rows, imag_rows], 1), "grid", scatter_dimension=0, tiled=True
            )
        )
    hamiltonian = jnp.stack(blocks, 1)
    hamiltonian = jnp.transpose(hamiltonian, (1, 0, 2))
    ham_real = hamiltonian[:, :, :half]
    ham_imag = hamiltonian[:, :, half:]
    row_index = lax.axis_index("grid") * share + lax.iota(jnp.int32, share)
    col_index = lax.iota(jnp.int32, half)
    identity = (row_index[:, None] == col_index[None, :]).astype(jnp.float32)[None]
    trace_part = jnp.sum(ham_real * identity, axis=(1, 2))
    trace = lax.psum(trace_part, "grid")
    level = (trace / half)[:, None, None]
    centred = ham_real - level * identity
    squares = jnp.sum(centred * centred, axis=(1, 2)) + jnp.sum(ham_imag * ham_imag, axis=(1, 2))
    total = lax.psum(squares, "grid")
    spread = jnp.sqrt(total / half + 1e-06)[:, None, None]
    filling = (occupied.astype(jnp.float32) / half)[:, None, None]
    dens_real = filling * identity - centred / (4.0 * spread)
    dens_imag = -ham_imag / (4.0 * spread)
    density = jnp.concatenate([dens_real, dens_imag], 2).astype(jnp.bfloat16)
    for repeat in range(MCW):
        gathered = lax.all_gather(density, "grid", axis=1, tiled=True)
        matrix = embedding(gathered)
        square = jnp.einsum("krc,kcd->krd", density, matrix, preferred_element_type=jnp.float32)
        cube = jnp.einsum(
            "krc,kcd->krd", square.astype(jnp.bfloat16), matrix, preferred_element_type=jnp.float32
        )
        density = (3.0 * square - 2.0 * cube).astype(jnp.bfloat16)
    gathered = lax.all_gather(density, "grid", axis=1, tiled=True)
    matrix = embedding(gathered)
    updated = jnp.einsum("kgc,kcd->kgd", bands, matrix, preferred_element_type=jnp.float32)
    return updated.astype(jnp.bfloat16)


def on_device(bands, hbands, occupied):
    points, rows, columns = bands.shape
    half = columns // 2
    if (
        lax.axis_size("grid") == 2 * CHIPS
        and points == 2
        and half % TILE == 0
        and half % (16 * CHIPS) == 0
    ):
        return fused(bands, hbands, occupied)
    return spread_out(bands, hbands, occupied)


def solution(mesh):
    return jax.shard_map(
        on_device,
        mesh=mesh,
        in_specs=(P("kset", "grid", None), P("kset", "grid", None), P("kset")),
        out_specs=P("kset", "grid", None),
        check_vma=False,
    )
```

```python
import functools

import jax
import jax.numpy as jnp
from jax import lax
from jax.experimental import pallas as pl
from jax.experimental.pallas import tpu as pltpu
from jax.sharding import PartitionSpec as P

MCW = 2
LINE = 4
CHIPS = 2 * LINE
TILE = 256
CHUNK = 128
PERIOD = 3
LAG = 2
MESH = pl.DeviceIdType.MESH


def dot_t(left, right):
    return lax.dot_general(
        left, right, (((0,), (0,)), ((), ())), preferred_element_type=jnp.float32
    )


def dot(left, right):
    return jnp.dot(left, right, preferred_element_type=jnp.float32)


def kernel(
    scale,
    occ_ref,
    bands_ref,
    hbands_ref,
    out_ref,
    mb,
    mh,
    nb,
    nh,
    rb,
    t_out,
    t_in,
    packed,
    s1,
    r1,
    s2,
    r2,
    s3,
    r3,
    dl,
    d_out,
    d_in,
    dr,
    full,
    re0,
    im0,
    m0,
    re1,
    im1,
    m1,
    sr,
    si,
    sum_m,
    sum_r,
    ob,
    in_send,
    in_recv,
    t_send,
    t_recv,
    ds_sem,
    dr_sem,
    c_send,
    c_recv,
    o_send,
    o_recv,
    load_sem,
):
    rows = bands_ref.shape[1]
    half = bands_ref.shape[2] // 2
    tiles = half // TILE
    count = half // CHUNK
    kset = lax.axis_index("kset")
    me = lax.axis_index("grid")
    core = lax.rem(me, 2)
    chip = me // 2
    x = lax.rem(chip, 2)
    z = chip // 2

    def device(chip_id, core_id):
        return (kset, chip_id * 2 + core_id)

    mate = device(chip, 1 - core)
    across = device(z * 2 + 1 - x, core)
    parity = lax.rem(z, 2)
    pair = device((z + 1 - 2 * parity) * 2 + x, core)
    cross = device(lax.rem(z + 2, LINE) * 2 + x, core)

    def remote(src, dst, send, recv, target):
        return pltpu.make_async_remote_copy(
            src_ref=src,
            dst_ref=dst,
            send_sem=send,
            recv_sem=recv,
            device_id=target,
            device_id_type=MESH,
        )

    loads = [
        pltpu.make_async_copy(source.at[point], target, load_sem.at[n])
        for n, (source, point, target) in enumerate(
            (
                (bands_ref, 1 - core, nb),
                (hbands_ref, 1 - core, nh),
                (bands_ref, core, mb),
                (hbands_ref, core, mh),
            )
        )
    ]
    for load in loads:
        load.start()
    barrier = pltpu.get_barrier_semaphore()
    pl.semaphore_signal(barrier, inc=1, device_id=mate, device_id_type=MESH)
    for r in range(1, CHIPS):
        pl.semaphore_signal(
            barrier, inc=1, device_id=device(lax.rem(chip + r, CHIPS), core), device_id_type=MESH
        )

    def project(band, hband, i, store):
        lo, hi = i * TILE, (i + 1) * TILE
        a_i = band[:, lo:hi]
        b_i = band[:, half + lo : half + hi]
        ha_i = hband[:, lo:hi]
        hb_i = hband[:, half + lo : half + hi]
        diag_r = dot_t(a_i, ha_i) + dot_t(b_i, hb_i)
        diag_i = dot_t(a_i, hb_i) - dot_t(b_i, ha_i)
        square_r = (diag_r + diag_r.T) * scale
        square_i = (diag_i - diag_i.T) * scale
        r_id = lax.broadcasted_iota(jnp.int32, (TILE, TILE), 0)
        c_id = lax.broadcasted_iota(jnp.int32, (TILE, TILE), 1)
        diag = jnp.sum(jnp.where(r_id == c_id, square_r, 0.0), axis=0, keepdims=True)
        mixed = jnp.where(r_id < c_id, square_r, jnp.where(r_id > c_id, square_i, 0.0))
        pieces = [(lo, hi, mixed)]
        if lo > 0:
            imag = (
                dot_t(a_i, hband[:, half : half + lo])
                + dot_t(ha_i, band[:, half : half + lo])
                - dot_t(b_i, hband[:, :lo])
                - dot_t(hb_i, band[:, :lo])
            ) * scale
            pieces.append((0, lo, imag))
        if hi < half:
            real = (
                dot_t(a_i, hband[:, hi:half])
                + dot_t(b_i, hband[:, half + hi :])
                + dot_t(ha_i, band[:, hi:half])
                + dot_t(hb_i, band[:, half + hi :])
            ) * scale
            pieces.append((hi, half, real))
        for c0, c1, value in pieces:
            store(i, slice(c0, c1), value)
        return diag

    copies = {}

    def send(c, stage, src, dst, target):
        copies[c, stage] = remote(src, dst, c_send.at[c, stage], c_recv.at[c, stage], target)
        copies[c, stage].start()

    def places(c):
        half_rows, quarter = CHUNK // 2, CHUNK // 4
        if c % PERIOD == PERIOD - 1:
            first, second, near, far = parity, x, pair, across
        else:
            first, second, near, far = x, parity, across, pair
        mine = c * CHUNK + first * half_rows
        other = c * CHUNK + (1 - first) * half_rows
        own = second * quarter
        rest = (1 - second) * quarter
        return mine, other, own, rest, near, far

    def span(start, size):
        return pl.ds(pl.multiple_of(start, 16), size)

    def begin(c):
        mine, other, own, rest, near, far = places(c)
        s1[c] = packed[span(other, CHUNK // 2), :].astype(jnp.bfloat16)
        send(c, 0, s1.at[c], r1.at[c], near)

    def advance(c, stage):
        mine, other, own, rest, near, far = places(c)
        quarter = CHUNK // 4
        copies[c, stage].wait_recv()
        if stage == 0:
            s2[c] = (
                packed[span(mine + rest, quarter), :]
                + r1[c, span(rest, quarter), :].astype(jnp.float32)
            ).astype(jnp.bfloat16)
            send(c, 1, s2.at[c], r2.at[c], far)
            packed[span(mine + own, quarter), :] = packed[span(mine + own, quarter), :] + r1[
                c, span(own, quarter), :
            ].astype(jnp.float32)
        elif stage == 1:
            value = packed[span(mine + own, quarter), :] + r2[c].astype(jnp.float32)
            s3[c] = value.astype(jnp.bfloat16)
            send(c, 2, s3.at[c], r3.at[c], cross)
            packed[span(mine + own, quarter), :] = value
        elif stage == 2:
            value = packed[span(mine + own, quarter), :] + r3[c].astype(jnp.float32)
            ready = full.at[span(mine + own, quarter), :]
            full[span(mine + own, quarter), :] = value.astype(jnp.bfloat16)
            send(c, 3, ready, ready, far)
            send(c, 4, ready, ready, near)
        elif stage == 3:
            ready = full.at[span(mine + rest, quarter), :]
            send(c, 5, ready, ready, near)

    per_tile = TILE // CHUNK
    handed = [
        remote(t_out.at[i], t_in.at[i], t_send.at[i], t_recv.at[i], mate) for i in range(tiles)
    ]

    def store_theirs(i, columns, value):
        t_out[i, :, columns] = value.astype(jnp.bfloat16)

    def store_own(i, columns, value):
        packed[i * TILE : (i + 1) * TILE, columns] = value + t_in[i, :, columns].astype(jnp.float32)

    def hand(i):
        d_out[:, i * TILE : (i + 1) * TILE] = project(nb, nh, i, store_theirs)

    def keep(i):
        handed[i].wait_recv()
        dl[:, i * TILE : (i + 1) * TILE] = project(mb, mh, i, store_own)
        for c in range(i * per_tile, (i + 1) * per_tile):
            begin(c)

    per_tile = TILE // CHUNK
    loads[0].wait()
    loads[1].wait()
    hand(0)
    pl.semaphore_wait(barrier, CHIPS)
    handed[0].start()
    loads[2].wait()
    loads[3].wait()
    for i in range(1, tiles):
        hand(i)
        handed[i].start()
        keep(i - 1)
    swap_d = remote(d_out, d_in, in_send.at[1], in_recv.at[1], mate)
    swap_d.start()
    swap_b = remote(nb, rb, in_send.at[0], in_recv.at[0], mate)
    swap_b.start()
    keep(tiles - 1)
    swap_d.wait()
    dl[...] = dl[...] + d_in[...]
    traces = []
    for r in range(1, CHIPS):
        copy = remote(
            dl,
            dr.at[r - 1],
            ds_sem.at[r - 1],
            dr_sem.at[r - 1],
            device(lax.rem(chip + r, CHIPS), core),
        )
        copy.start()
        traces.append(copy)
    events = sorted((c + LAG * stage, stage, c) for c in range(count) for stage in range(4))
    for n, (_, stage, c) in enumerate(events):
        advance(c, stage)
        if n == count:
            sum_m[...] = mb[:, :half] + mb[:, half:]
        if n == 2 * count:
            swap_b.wait()
            sum_r[...] = rb[:, :half] + rb[:, half:]
    for c in range(count):
        copies[c, 4].wait_recv()
        copies[c, 5].wait_recv()
    diag = dl[...]
    for r in range(1, CHIPS):
        traces[r - 1].wait()
        diag = diag + dr[r - 1]

    level = jnp.sum(diag, axis=1, keepdims=True) / half
    centred = diag - level
    total = jnp.sum(centred * centred, axis=1, keepdims=True)
    square_sum = jnp.zeros((1, half), jnp.float32)
    for i in range(tiles):
        block = full[i * TILE : (i + 1) * TILE, :].astype(jnp.float32)
        square_sum = square_sum + jnp.sum(block * block, axis=0, keepdims=True)
    total = total + 2.0 * jnp.sum(square_sum, axis=1, keepdims=True)
    spread = jnp.sqrt(total / half + 1e-06)
    factor = 1.0 / (4.0 * spread)
    filling = occ_ref[core].astype(jnp.float32) / half
    on_diag = filling - centred * factor
    for i in range(tiles):
        rows_i = slice(i * TILE, (i + 1) * TILE)
        r_id = lax.broadcasted_iota(jnp.int32, (TILE, TILE), 0)
        c_id = lax.broadcasted_iota(jnp.int32, (TILE, TILE), 1)
        block = full[rows_i, rows_i].astype(jnp.float32) * factor
        turned = block.T
        re0[rows_i, rows_i] = jnp.where(
            r_id == c_id, on_diag[:, rows_i], jnp.where(r_id < c_id, -block, -turned)
        ).astype(jnp.bfloat16)
        im0[rows_i, rows_i] = jnp.where(r_id > c_id, -block, turned).astype(jnp.bfloat16)
        for j in range(i + 1, tiles):
            rows_j = slice(j * TILE, (j + 1) * TILE)
            upper = full[rows_i, rows_j].astype(jnp.float32) * factor
            lower = full[rows_j, rows_i].astype(jnp.float32) * factor
            re0[rows_i, rows_j] = (-upper).astype(jnp.bfloat16)
            re0[rows_j, rows_i] = (-upper.T).astype(jnp.bfloat16)
            im0[rows_j, rows_i] = (-lower).astype(jnp.bfloat16)
            im0[rows_i, rows_j] = lower.T.astype(jnp.bfloat16)

    def three(left, right):
        p = dot(left[0], right[0])
        q = dot(left[1], right[1])
        return p - q, dot(left[2], right[2]) - (p + q)

    def mirror(i, refs, real, imag):
        lo = i * TILE
        real, imag = real.astype(jnp.bfloat16), imag.astype(jnp.bfloat16)
        own_rows, right = slice(lo, lo + TILE), slice(lo, half)
        places = [(own_rows, right, real, imag)]
        for k in range(1, tiles - i):
            part = slice(k * TILE, (k + 1) * TILE)
            below = slice(lo + k * TILE, lo + (k + 1) * TILE)
            places.append((below, own_rows, real[:, part].T, -imag[:, part].T))
        for down, along, r, i in places:
            for ref, value in zip(refs, (r, i, r + i)):
                ref[down, along] = value

    def purify(now, following):
        for i in range(tiles):
            lo = i * TILE
            own_rows = slice(lo, lo + TILE)
            right = slice(lo, half)
            columns = [ref[:, right] for ref in now]
            sq_r, sq_i = three([ref[own_rows, :] for ref in now], columns)
            mirror(i, (sr, si), sq_r, sq_i)
            s_r, s_i = sr[own_rows, :], si[own_rows, :]
            cube_r, cube_i = three([s_r, s_i, s_r + s_i], columns)
            mirror(i, following, 3.0 * sq_r - 2.0 * cube_r, 3.0 * sq_i - 2.0 * cube_i)

    m0[...] = re0[...] + im0[...]
    bufs = [(re0, im0, m0), (re1, im1, m1)]
    for step in range(MCW):
        purify(bufs[step % 2], bufs[(step + 1) % 2])
    last = [ref[...] for ref in bufs[MCW % 2]]

    def update(band, band_sum, target):
        real, imag = three([band[:, :half], band[:, half:], band_sum[...]], last)
        target[:, :half] = real.astype(jnp.bfloat16)
        target[:, half:] = imag.astype(jnp.bfloat16)

    backs = []
    for n in range(2):
        part = slice(n * rows // 2, (n + 1) * rows // 2)
        update(rb.at[part, :], sum_r.at[part, :], ob.at[part, :])
        back = remote(
            ob.at[part, :], out_ref.at[core, part, :], o_send.at[n], o_recv.at[n], mate
        )
        back.start()
        backs.append(back)
    update(mb, sum_m, out_ref.at[core])
    for back in backs:
        back.wait()
    for copy in handed:
        copy.wait_send()
    for copy in copies.values():
        copy.wait_send()


def fused(bands, hbands, occupied):
    points, rows, columns = bands.shape
    half = columns // 2
    count = half // CHUNK
    scale = 1.0 / (2.0 * rows * lax.axis_size("grid"))
    bf16, f32 = jnp.bfloat16, jnp.float32
    dma = pltpu.SemaphoreType.DMA
    return pl.pallas_call(
        functools.partial(kernel, scale),
        out_shape=pltpu.VMEM(bands.shape, bf16),
        in_specs=[
            pl.BlockSpec(memory_space=pltpu.SMEM),
            pl.BlockSpec(memory_space=pltpu.HBM),
            pl.BlockSpec(memory_space=pltpu.HBM),
        ],
        out_specs=pl.BlockSpec(memory_space=pltpu.VMEM),
        scratch_shapes=[
            pltpu.VMEM((rows, columns), bf16),
            pltpu.VMEM((rows, columns), bf16),
            pltpu.VMEM((rows, columns), bf16),
            pltpu.VMEM((rows, columns), bf16),
            pltpu.VMEM((rows, columns), bf16),
            pltpu.VMEM((half // TILE, TILE, half), bf16),
            pltpu.VMEM((half // TILE, TILE, half), bf16),
            pltpu.VMEM((half, half), f32),
            pltpu.VMEM((count, CHUNK // 2, half), bf16),
            pltpu.VMEM((count, CHUNK // 2, half), bf16),
            pltpu.VMEM((count, CHUNK // 4, half), bf16),
            pltpu.VMEM((count, CHUNK // 4, half), bf16),
            pltpu.VMEM((count, CHUNK // 4, half), bf16),
            pltpu.VMEM((count, CHUNK // 4, half), bf16),
            pltpu.VMEM((1, half), f32),
            pltpu.VMEM((1, half), f32),
            pltpu.VMEM((1, half), f32),
            pltpu.VMEM((CHIPS - 1, 1, half), f32),
            pltpu.VMEM((half, half), bf16),
            pltpu.VMEM((half, half), bf16),
            pltpu.VMEM((half, half), bf16),
            pltpu.VMEM((half, half), bf16),
            pltpu.VMEM((half, half), bf16),
            pltpu.VMEM((half, half), bf16),
            pltpu.VMEM((half, half), bf16),
            pltpu.VMEM((half, half), bf16),
            pltpu.VMEM((half, half), bf16),
            pltpu.VMEM((rows, half), bf16),
            pltpu.VMEM((rows, half), bf16),
            pltpu.VMEM((rows, columns), bf16),
            dma((2,)),
            dma((2,)),
            dma((half // TILE,)),
            dma((half // TILE,)),
            dma((CHIPS - 1,)),
            dma((CHIPS - 1,)),
            dma((count, 6)),
            dma((count, 6)),
            dma((2,)),
            dma((2,)),
            dma((4,)),
        ],
        compiler_params=pltpu.CompilerParams(
            collective_id=0, has_side_effects=True, vmem_limit_bytes=40 * 1024 * 1024
        ),
    )(*(pltpu.with_memory_space_constraint(x, pltpu.HBM) for x in (occupied, bands, hbands)))


def embedding(full):
    width = full.shape[-1] // 2
    real_part = full[..., :width]
    imag_part = full[..., width:]
    upper = jnp.concatenate([real_part, imag_part], -1)
    lower = jnp.concatenate([-imag_part, real_part], -1)
    return jnp.concatenate([upper, lower], -2)


def spread_out(bands, hbands, occupied):
    points, local_rows, columns = bands.shape
    half = columns // 2
    devices = lax.axis_size("grid")
    share = half // devices
    scale = 1.0 / (2.0 * local_rows * devices)
    blocks = []
    for point in range(points):
        start = jnp.int32(0)
        count = lax.axis_size("grid") * share
        band_k = bands[point]
        hband_k = hbands[point]
        band_cols = jnp.concatenate(
            [
                lax.dynamic_slice_in_dim(band_k, start, count, 1),
                lax.dynamic_slice_in_dim(band_k, half, count, 1),
            ],
            1,
        )
        summed = jnp.einsum("gi,gj->ij", band_cols, hband_k, preferred_element_type=jnp.float32)
        hband_cols = jnp.concatenate(
            [
                lax.dynamic_slice_in_dim(hband_k, start, count, 1),
                lax.dynamic_slice_in_dim(hband_k, half, count, 1),
            ],
            1,
        )
        summed = summed + jnp.einsum(
            "gi,gj->ij", hband_cols, band_k, preferred_element_type=jnp.float32
        )
        real_rows = (summed[:count, :half] + summed[count:, half:]) * scale
        imag_rows = (summed[:count, half:] - summed[count:, :half]) * scale
        blocks.append(
            lax.psum_scatter(
                jnp.concatenate([real_rows, imag_rows], 1), "grid", scatter_dimension=0, tiled=True
            )
        )
    hamiltonian = jnp.stack(blocks, 1)
    hamiltonian = jnp.transpose(hamiltonian, (1, 0, 2))
    ham_real = hamiltonian[:, :, :half]
    ham_imag = hamiltonian[:, :, half:]
    row_index = lax.axis_index("grid") * share + lax.iota(jnp.int32, share)
    col_index = lax.iota(jnp.int32, half)
    identity = (row_index[:, None] == col_index[None, :]).astype(jnp.float32)[None]
    trace_part = jnp.sum(ham_real * identity, axis=(1, 2))
    trace = lax.psum(trace_part, "grid")
    level = (trace / half)[:, None, None]
    centred = ham_real - level * identity
    squares = jnp.sum(centred * centred, axis=(1, 2)) + jnp.sum(ham_imag * ham_imag, axis=(1, 2))
    total = lax.psum(squares, "grid")
    spread = jnp.sqrt(total / half + 1e-06)[:, None, None]
    filling = (occupied.astype(jnp.float32) / half)[:, None, None]
    dens_real = filling * identity - centred / (4.0 * spread)
    dens_imag = -ham_imag / (4.0 * spread)
    density = jnp.concatenate([dens_real, dens_imag], 2).astype(jnp.bfloat16)
    for repeat in range(MCW):
        gathered = lax.all_gather(density, "grid", axis=1, tiled=True)
        matrix = embedding(gathered)
        square = jnp.einsum("krc,kcd->krd", density, matrix, preferred_element_type=jnp.float32)
        cube = jnp.einsum(
            "krc,kcd->krd", square.astype(jnp.bfloat16), matrix, preferred_element_type=jnp.float32
        )
        density = (3.0 * square - 2.0 * cube).astype(jnp.bfloat16)
    gathered = lax.all_gather(density, "grid", axis=1, tiled=True)
    matrix = embedding(gathered)
    updated = jnp.einsum("kgc,kcd->kgd", bands, matrix, preferred_element_type=jnp.float32)
    return updated.astype(jnp.bfloat16)


def on_device(bands, hbands, occupied):
    points, rows, columns = bands.shape
    half = columns // 2
    if (
        lax.axis_size("grid") == 2 * CHIPS
        and points == 2
        and half % TILE == 0
        and half % (16 * CHIPS) == 0
    ):
        return fused(bands, hbands, occupied)
    return spread_out(bands, hbands, occupied)


def solution(mesh):
    return jax.shard_map(
        on_device,
        mesh=mesh,
        in_specs=(P("kset", "grid", None), P("kset", "grid", None), P("kset")),
        out_specs=P("kset", "grid", None),
        check_vma=False,
    )
```

```python
import functools

import jax
import jax.numpy as jnp
from jax import lax
from jax.experimental import pallas as pl
from jax.experimental.pallas import tpu as pltpu
from jax.sharding import PartitionSpec as P

MCW = 2
LINE = 4
CHIPS = 2 * LINE
TILE = 256
CHUNK = 128
PERIOD = 3
LAG = 2
MESH = pl.DeviceIdType.MESH


def dot_t(left, right):
    return lax.dot_general(
        left, right, (((0,), (0,)), ((), ())), preferred_element_type=jnp.float32
    )


def dot(left, right):
    return jnp.dot(left, right, preferred_element_type=jnp.float32)


def kernel(
    scale,
    occ_ref,
    bands_ref,
    hbands_ref,
    out_ref,
    mb,
    mh,
    nb,
    nh,
    rb,
    t_out,
    t_in,
    packed,
    s1,
    r1,
    s2,
    r2,
    s3,
    r3,
    dl,
    d_out,
    d_in,
    dr,
    full,
    re0,
    im0,
    m0,
    re1,
    im1,
    m1,
    sr,
    si,
    sum_m,
    sum_r,
    ob,
    in_send,
    in_recv,
    t_send,
    t_recv,
    ds_sem,
    dr_sem,
    c_send,
    c_recv,
    o_send,
    o_recv,
    load_sem,
):
    rows = bands_ref.shape[1]
    half = bands_ref.shape[2] // 2
    tiles = half // TILE
    count = half // CHUNK
    kset = lax.axis_index("kset")
    me = lax.axis_index("grid")
    core = lax.rem(me, 2)
    chip = me // 2
    x = lax.rem(chip, 2)
    z = chip // 2

    def device(chip_id, core_id):
        return (kset, chip_id * 2 + core_id)

    mate = device(chip, 1 - core)
    across = device(z * 2 + 1 - x, core)
    parity = lax.rem(z, 2)
    pair = device((z + 1 - 2 * parity) * 2 + x, core)
    cross = device(lax.rem(z + 2, LINE) * 2 + x, core)

    def remote(src, dst, send, recv, target):
        return pltpu.make_async_remote_copy(
            src_ref=src,
            dst_ref=dst,
            send_sem=send,
            recv_sem=recv,
            device_id=target,
            device_id_type=MESH,
        )

    loads = [
        pltpu.make_async_copy(source.at[point], target, load_sem.at[n])
        for n, (source, point, target) in enumerate(
            (
                (bands_ref, 1 - core, nb),
                (hbands_ref, 1 - core, nh),
                (bands_ref, core, mb),
                (hbands_ref, core, mh),
            )
        )
    ]
    for load in loads:
        load.start()
    barrier = pltpu.get_barrier_semaphore()
    pl.semaphore_signal(barrier, inc=1, device_id=mate, device_id_type=MESH)
    for r in range(1, CHIPS):
        pl.semaphore_signal(
            barrier, inc=1, device_id=device(lax.rem(chip + r, CHIPS), core), device_id_type=MESH
        )

    def project(band, hband, i, store):
        lo, hi = i * TILE, (i + 1) * TILE
        a_i = band[:, lo:hi]
        b_i = band[:, half + lo : half + hi]
        ha_i = hband[:, lo:hi]
        hb_i = hband[:, half + lo : half + hi]
        diag_r = dot_t(a_i, ha_i) + dot_t(b_i, hb_i)
        diag_i = dot_t(a_i, hb_i) - dot_t(b_i, ha_i)
        square_r = (diag_r + diag_r.T) * scale
        square_i = (diag_i - diag_i.T) * scale
        r_id = lax.broadcasted_iota(jnp.int32, (TILE, TILE), 0)
        c_id = lax.broadcasted_iota(jnp.int32, (TILE, TILE), 1)
        diag = jnp.sum(jnp.where(r_id == c_id, square_r, 0.0), axis=0, keepdims=True)
        mixed = jnp.where(r_id < c_id, square_r, jnp.where(r_id > c_id, square_i, 0.0))
        pieces = [(lo, hi, mixed)]
        if lo > 0:
            imag = (
                dot_t(a_i, hband[:, half : half + lo])
                + dot_t(ha_i, band[:, half : half + lo])
                - dot_t(b_i, hband[:, :lo])
                - dot_t(hb_i, band[:, :lo])
            ) * scale
            pieces.append((0, lo, imag))
        if hi < half:
            real = (
                dot_t(a_i, hband[:, hi:half])
                + dot_t(b_i, hband[:, half + hi :])
                + dot_t(ha_i, band[:, hi:half])
                + dot_t(hb_i, band[:, half + hi :])
            ) * scale
            pieces.append((hi, half, real))
        for c0, c1, value in pieces:
            store(i, slice(c0, c1), value)
        return diag

    copies = {}

    def send(c, stage, src, dst, target):
        copies[c, stage] = remote(src, dst, c_send.at[c, stage], c_recv.at[c, stage], target)
        copies[c, stage].start()

    def places(c):
        half_rows, quarter = CHUNK // 2, CHUNK // 4
        if c % PERIOD == PERIOD - 1:
            first, second, near, far = parity, x, pair, across
        else:
            first, second, near, far = x, parity, across, pair
        mine = c * CHUNK + first * half_rows
        other = c * CHUNK + (1 - first) * half_rows
        own = second * quarter
        rest = (1 - second) * quarter
        return mine, other, own, rest, near, far

    def span(start, size):
        return pl.ds(pl.multiple_of(start, 16), size)

    def begin(c):
        mine, other, own, rest, near, far = places(c)
        s1[c] = packed[span(other, CHUNK // 2), :].astype(jnp.bfloat16)
        send(c, 0, s1.at[c], r1.at[c], near)

    def advance(c, stage):
        mine, other, own, rest, near, far = places(c)
        quarter = CHUNK // 4
        copies[c, stage].wait_recv()
        if stage == 0:
            s2[c] = (
                packed[span(mine + rest, quarter), :]
                + r1[c, span(rest, quarter), :].astype(jnp.float32)
            ).astype(jnp.bfloat16)
            send(c, 1, s2.at[c], r2.at[c], far)
            packed[span(mine + own, quarter), :] = packed[span(mine + own, quarter), :] + r1[
                c, span(own, quarter), :
            ].astype(jnp.float32)
        elif stage == 1:
            value = packed[span(mine + own, quarter), :] + r2[c].astype(jnp.float32)
            s3[c] = value.astype(jnp.bfloat16)
            send(c, 2, s3.at[c], r3.at[c], cross)
            packed[span(mine + own, quarter), :] = value
        elif stage == 2:
            value = packed[span(mine + own, quarter), :] + r3[c].astype(jnp.float32)
            ready = full.at[span(mine + own, quarter), :]
            full[span(mine + own, quarter), :] = value.astype(jnp.bfloat16)
            send(c, 4, ready, ready, near)
            send(c, 3, ready, ready, far)
        elif stage == 3:
            ready = full.at[span(mine + rest, quarter), :]
            send(c, 5, ready, ready, near)

    per_tile = TILE // CHUNK
    handed = [
        remote(t_out.at[i], t_in.at[i], t_send.at[i], t_recv.at[i], mate) for i in range(tiles)
    ]

    def store_theirs(i, columns, value):
        t_out[i, :, columns] = value.astype(jnp.bfloat16)

    def store_own(i, columns, value):
        packed[i * TILE : (i + 1) * TILE, columns] = value + t_in[i, :, columns].astype(jnp.float32)

    def hand(i):
        d_out[:, i * TILE : (i + 1) * TILE] = project(nb, nh, i, store_theirs)

    def keep(i):
        handed[i].wait_recv()
        dl[:, i * TILE : (i + 1) * TILE] = project(mb, mh, i, store_own)
        for c in range(i * per_tile, (i + 1) * per_tile):
            begin(c)

    per_tile = TILE // CHUNK
    loads[0].wait()
    loads[1].wait()
    hand(0)
    pl.semaphore_wait(barrier, CHIPS)
    handed[0].start()
    loads[2].wait()
    loads[3].wait()
    for i in range(1, tiles):
        hand(i)
        handed[i].start()
        keep(i - 1)
    swap_d = remote(d_out, d_in, in_send.at[1], in_recv.at[1], mate)
    swap_d.start()
    swap_b = remote(nb, rb, in_send.at[0], in_recv.at[0], mate)
    swap_b.start()
    keep(tiles - 1)
    swap_d.wait()
    dl[...] = dl[...] + d_in[...]
    traces = []
    for r in range(1, CHIPS):
        copy = remote(
            dl,
            dr.at[r - 1],
            ds_sem.at[r - 1],
            dr_sem.at[r - 1],
            device(lax.rem(chip + r, CHIPS), core),
        )
        copy.start()
        traces.append(copy)
    events = sorted((c + LAG * stage, stage, c) for c in range(count) for stage in range(4))
    for n, (_, stage, c) in enumerate(events):
        advance(c, stage)
        if n == count:
            sum_m[...] = mb[:, :half] + mb[:, half:]
        if n == 2 * count:
            swap_b.wait()
            sum_r[...] = rb[:, :half] + rb[:, half:]
    diag = dl[...]
    for r in range(1, CHIPS):
        traces[r - 1].wait()
        diag = diag + dr[r - 1]
    square_sum = jnp.zeros((1, half), jnp.float32)
    for c in range(count):
        copies[c, 4].wait_recv()
        copies[c, 5].wait_recv()
        block = full[c * CHUNK : (c + 1) * CHUNK, :].astype(jnp.float32)
        square_sum = square_sum + jnp.sum(block * block, axis=0, keepdims=True)
    level = jnp.sum(diag, axis=1, keepdims=True) / half
    centred = diag - level
    total = jnp.sum(centred * centred, axis=1, keepdims=True)
    total = total + 2.0 * jnp.sum(square_sum, axis=1, keepdims=True)
    spread = jnp.sqrt(total / half + 1e-06)
    factor = 1.0 / (4.0 * spread)
    filling = occ_ref[core].astype(jnp.float32) / half
    on_diag = filling - centred * factor
    for i in range(tiles):
        rows_i = slice(i * TILE, (i + 1) * TILE)
        r_id = lax.broadcasted_iota(jnp.int32, (TILE, TILE), 0)
        c_id = lax.broadcasted_iota(jnp.int32, (TILE, TILE), 1)
        block = full[rows_i, rows_i].astype(jnp.float32) * factor
        turned = block.T
        re0[rows_i, rows_i] = jnp.where(
            r_id == c_id, on_diag[:, rows_i], jnp.where(r_id < c_id, -block, -turned)
        ).astype(jnp.bfloat16)
        im0[rows_i, rows_i] = jnp.where(r_id > c_id, -block, turned).astype(jnp.bfloat16)
        for j in range(i + 1, tiles):
            rows_j = slice(j * TILE, (j + 1) * TILE)
            upper = full[rows_i, rows_j].astype(jnp.float32) * factor
            lower = full[rows_j, rows_i].astype(jnp.float32) * factor
            re0[rows_i, rows_j] = (-upper).astype(jnp.bfloat16)
            re0[rows_j, rows_i] = (-upper.T).astype(jnp.bfloat16)
            im0[rows_j, rows_i] = (-lower).astype(jnp.bfloat16)
            im0[rows_i, rows_j] = lower.T.astype(jnp.bfloat16)

    def three(left, right):
        p = dot(left[0], right[0])
        q = dot(left[1], right[1])
        return p - q, dot(left[2], right[2]) - (p + q)

    def mirror(i, refs, real, imag):
        lo = i * TILE
        real, imag = real.astype(jnp.bfloat16), imag.astype(jnp.bfloat16)
        own_rows, right = slice(lo, lo + TILE), slice(lo, half)
        places = [(own_rows, right, real, imag)]
        for k in range(1, tiles - i):
            part = slice(k * TILE, (k + 1) * TILE)
            below = slice(lo + k * TILE, lo + (k + 1) * TILE)
            places.append((below, own_rows, real[:, part].T, -imag[:, part].T))
        for down, along, r, i in places:
            for ref, value in zip(refs, (r, i, r + i)):
                ref[down, along] = value

    def purify(now, following):
        for i in range(tiles):
            lo = i * TILE
            own_rows = slice(lo, lo + TILE)
            right = slice(lo, half)
            columns = [ref[:, right] for ref in now]
            sq_r, sq_i = three([ref[own_rows, :] for ref in now], columns)
            mirror(i, (sr, si), sq_r, sq_i)
            s_r, s_i = sr[own_rows, :], si[own_rows, :]
            cube_r, cube_i = three([s_r, s_i, s_r + s_i], columns)
            mirror(i, following, 3.0 * sq_r - 2.0 * cube_r, 3.0 * sq_i - 2.0 * cube_i)

    m0[...] = re0[...] + im0[...]
    bufs = [(re0, im0, m0), (re1, im1, m1)]
    for step in range(MCW):
        purify(bufs[step % 2], bufs[(step + 1) % 2])
    last = [ref[...] for ref in bufs[MCW % 2]]

    def update(band, band_sum, target):
        real, imag = three([band[:, :half], band[:, half:], band_sum[...]], last)
        target[:, :half] = real.astype(jnp.bfloat16)
        target[:, half:] = imag.astype(jnp.bfloat16)

    backs = []
    for n in range(2):
        part = slice(n * rows // 2, (n + 1) * rows // 2)
        update(rb.at[part, :], sum_r.at[part, :], ob.at[part, :])
        back = remote(
            ob.at[part, :], out_ref.at[core, part, :], o_send.at[n], o_recv.at[n], mate
        )
        back.start()
        backs.append(back)
    update(mb, sum_m, out_ref.at[core])
    for back in backs:
        back.wait()
    for copy in handed:
        copy.wait_send()
    for copy in copies.values():
        copy.wait_send()


def fused(bands, hbands, occupied):
    points, rows, columns = bands.shape
    half = columns // 2
    count = half // CHUNK
    scale = 1.0 / (2.0 * rows * lax.axis_size("grid"))
    bf16, f32 = jnp.bfloat16, jnp.float32
    dma = pltpu.SemaphoreType.DMA
    return pl.pallas_call(
        functools.partial(kernel, scale),
        out_shape=pltpu.VMEM(bands.shape, bf16),
        in_specs=[
            pl.BlockSpec(memory_space=pltpu.SMEM),
            pl.BlockSpec(memory_space=pltpu.HBM),
            pl.BlockSpec(memory_space=pltpu.HBM),
        ],
        out_specs=pl.BlockSpec(memory_space=pltpu.VMEM),
        scratch_shapes=[
            pltpu.VMEM((rows, columns), bf16),
            pltpu.VMEM((rows, columns), bf16),
            pltpu.VMEM((rows, columns), bf16),
            pltpu.VMEM((rows, columns), bf16),
            pltpu.VMEM((rows, columns), bf16),
            pltpu.VMEM((half // TILE, TILE, half), bf16),
            pltpu.VMEM((half // TILE, TILE, half), bf16),
            pltpu.VMEM((half, half), f32),
            pltpu.VMEM((count, CHUNK // 2, half), bf16),
            pltpu.VMEM((count, CHUNK // 2, half), bf16),
            pltpu.VMEM((count, CHUNK // 4, half), bf16),
            pltpu.VMEM((count, CHUNK // 4, half), bf16),
            pltpu.VMEM((count, CHUNK // 4, half), bf16),
            pltpu.VMEM((count, CHUNK // 4, half), bf16),
            pltpu.VMEM((1, half), f32),
            pltpu.VMEM((1, half), f32),
            pltpu.VMEM((1, half), f32),
            pltpu.VMEM((CHIPS - 1, 1, half), f32),
            pltpu.VMEM((half, half), bf16),
            pltpu.VMEM((half, half), bf16),
            pltpu.VMEM((half, half), bf16),
            pltpu.VMEM((half, half), bf16),
            pltpu.VMEM((half, half), bf16),
            pltpu.VMEM((half, half), bf16),
            pltpu.VMEM((half, half), bf16),
            pltpu.VMEM((half, half), bf16),
            pltpu.VMEM((half, half), bf16),
            pltpu.VMEM((rows, half), bf16),
            pltpu.VMEM((rows, half), bf16),
            pltpu.VMEM((rows, columns), bf16),
            dma((2,)),
            dma((2,)),
            dma((half // TILE,)),
            dma((half // TILE,)),
            dma((CHIPS - 1,)),
            dma((CHIPS - 1,)),
            dma((count, 6)),
            dma((count, 6)),
            dma((2,)),
            dma((2,)),
            dma((4,)),
        ],
        compiler_params=pltpu.CompilerParams(
            collective_id=0, has_side_effects=True, vmem_limit_bytes=40 * 1024 * 1024
        ),
    )(*(pltpu.with_memory_space_constraint(x, pltpu.HBM) for x in (occupied, bands, hbands)))


def embedding(full):
    width = full.shape[-1] // 2
    real_part = full[..., :width]
    imag_part = full[..., width:]
    upper = jnp.concatenate([real_part, imag_part], -1)
    lower = jnp.concatenate([-imag_part, real_part], -1)
    return jnp.concatenate([upper, lower], -2)


def spread_out(bands, hbands, occupied):
    points, local_rows, columns = bands.shape
    half = columns // 2
    devices = lax.axis_size("grid")
    share = half // devices
    scale = 1.0 / (2.0 * local_rows * devices)
    blocks = []
    for point in range(points):
        start = jnp.int32(0)
        count = lax.axis_size("grid") * share
        band_k = bands[point]
        hband_k = hbands[point]
        band_cols = jnp.concatenate(
            [
                lax.dynamic_slice_in_dim(band_k, start, count, 1),
                lax.dynamic_slice_in_dim(band_k, half, count, 1),
            ],
            1,
        )
        summed = jnp.einsum("gi,gj->ij", band_cols, hband_k, preferred_element_type=jnp.float32)
        hband_cols = jnp.concatenate(
            [
                lax.dynamic_slice_in_dim(hband_k, start, count, 1),
                lax.dynamic_slice_in_dim(hband_k, half, count, 1),
            ],
            1,
        )
        summed = summed + jnp.einsum(
            "gi,gj->ij", hband_cols, band_k, preferred_element_type=jnp.float32
        )
        real_rows = (summed[:count, :half] + summed[count:, half:]) * scale
        imag_rows = (summed[:count, half:] - summed[count:, :half]) * scale
        blocks.append(
            lax.psum_scatter(
                jnp.concatenate([real_rows, imag_rows], 1), "grid", scatter_dimension=0, tiled=True
            )
        )
    hamiltonian = jnp.stack(blocks, 1)
    hamiltonian = jnp.transpose(hamiltonian, (1, 0, 2))
    ham_real = hamiltonian[:, :, :half]
    ham_imag = hamiltonian[:, :, half:]
    row_index = lax.axis_index("grid") * share + lax.iota(jnp.int32, share)
    col_index = lax.iota(jnp.int32, half)
    identity = (row_index[:, None] == col_index[None, :]).astype(jnp.float32)[None]
    trace_part = jnp.sum(ham_real * identity, axis=(1, 2))
    trace = lax.psum(trace_part, "grid")
    level = (trace / half)[:, None, None]
    centred = ham_real - level * identity
    squares = jnp.sum(centred * centred, axis=(1, 2)) + jnp.sum(ham_imag * ham_imag, axis=(1, 2))
    total = lax.psum(squares, "grid")
    spread = jnp.sqrt(total / half + 1e-06)[:, None, None]
    filling = (occupied.astype(jnp.float32) / half)[:, None, None]
    dens_real = filling * identity - centred / (4.0 * spread)
    dens_imag = -ham_imag / (4.0 * spread)
    density = jnp.concatenate([dens_real, dens_imag], 2).astype(jnp.bfloat16)
    for repeat in range(MCW):
        gathered = lax.all_gather(density, "grid", axis=1, tiled=True)
        matrix = embedding(gathered)
        square = jnp.einsum("krc,kcd->krd", density, matrix, preferred_element_type=jnp.float32)
        cube = jnp.einsum(
            "krc,kcd->krd", square.astype(jnp.bfloat16), matrix, preferred_element_type=jnp.float32
        )
        density = (3.0 * square - 2.0 * cube).astype(jnp.bfloat16)
    gathered = lax.all_gather(density, "grid", axis=1, tiled=True)
    matrix = embedding(gathered)
    updated = jnp.einsum("kgc,kcd->kgd", bands, matrix, preferred_element_type=jnp.float32)
    return updated.astype(jnp.bfloat16)


def on_device(bands, hbands, occupied):
    points, rows, columns = bands.shape
    half = columns // 2
    if (
        lax.axis_size("grid") == 2 * CHIPS
        and points == 2
        and half % TILE == 0
        and half % (16 * CHIPS) == 0
    ):
        return fused(bands, hbands, occupied)
    return spread_out(bands, hbands, occupied)


def solution(mesh):
    return jax.shard_map(
        on_device,
        mesh=mesh,
        in_specs=(P("kset", "grid", None), P("kset", "grid", None), P("kset")),
        out_specs=P("kset", "grid", None),
        check_vma=False,
    )
```

```python
import functools

import jax
import jax.numpy as jnp
from jax import lax
from jax.experimental import pallas as pl
from jax.experimental.pallas import tpu as pltpu
from jax.sharding import PartitionSpec as P

MCW = 2
LINE = 4
CHIPS = 2 * LINE
TILE = 256
CHUNK = 128
PERIOD = 3
LAGS = (0, 2, 4, 6.4)
MESH = pl.DeviceIdType.MESH


def dot_t(left, right):
    return lax.dot_general(
        left, right, (((0,), (0,)), ((), ())), preferred_element_type=jnp.float32
    )


def dot(left, right):
    return jnp.dot(left, right, preferred_element_type=jnp.float32)


def kernel(
    scale,
    occ_ref,
    bands_ref,
    hbands_ref,
    out_ref,
    mb,
    mh,
    nb,
    nh,
    rb,
    t_out,
    t_in,
    packed,
    s1,
    r1,
    s2,
    r2,
    s3,
    r3,
    dl,
    d_out,
    d_in,
    dr,
    full,
    re0,
    im0,
    m0,
    re1,
    im1,
    m1,
    sr,
    si,
    sum_m,
    sum_r,
    ob,
    in_send,
    in_recv,
    t_send,
    t_recv,
    ds_sem,
    dr_sem,
    c_send,
    c_recv,
    o_send,
    o_recv,
    load_sem,
):
    rows = bands_ref.shape[1]
    half = bands_ref.shape[2] // 2
    tiles = half // TILE
    count = half // CHUNK
    kset = lax.axis_index("kset")
    me = lax.axis_index("grid")
    core = lax.rem(me, 2)
    chip = me // 2
    x = lax.rem(chip, 2)
    z = chip // 2

    def device(chip_id, core_id):
        return (kset, chip_id * 2 + core_id)

    mate = device(chip, 1 - core)
    across = device(z * 2 + 1 - x, core)
    parity = lax.rem(z, 2)
    pair = device((z + 1 - 2 * parity) * 2 + x, core)
    cross = device(lax.rem(z + 2, LINE) * 2 + x, core)

    def remote(src, dst, send, recv, target):
        return pltpu.make_async_remote_copy(
            src_ref=src,
            dst_ref=dst,
            send_sem=send,
            recv_sem=recv,
            device_id=target,
            device_id_type=MESH,
        )

    loads = [
        pltpu.make_async_copy(source.at[point], target, load_sem.at[n])
        for n, (source, point, target) in enumerate(
            (
                (bands_ref, 1 - core, nb),
                (hbands_ref, 1 - core, nh),
                (bands_ref, core, mb),
                (hbands_ref, core, mh),
            )
        )
    ]
    for load in loads:
        load.start()
    barrier = pltpu.get_barrier_semaphore()
    pl.semaphore_signal(barrier, inc=1, device_id=mate, device_id_type=MESH)
    for r in range(1, CHIPS):
        pl.semaphore_signal(
            barrier, inc=1, device_id=device(lax.rem(chip + r, CHIPS), core), device_id_type=MESH
        )

    def project(band, hband, i, store):
        lo, hi = i * TILE, (i + 1) * TILE
        a_i = band[:, lo:hi]
        b_i = band[:, half + lo : half + hi]
        ha_i = hband[:, lo:hi]
        hb_i = hband[:, half + lo : half + hi]
        diag_r = dot_t(a_i, ha_i) + dot_t(b_i, hb_i)
        diag_i = dot_t(a_i, hb_i) - dot_t(b_i, ha_i)
        square_r = (diag_r + diag_r.T) * scale
        square_i = (diag_i - diag_i.T) * scale
        r_id = lax.broadcasted_iota(jnp.int32, (TILE, TILE), 0)
        c_id = lax.broadcasted_iota(jnp.int32, (TILE, TILE), 1)
        diag = jnp.sum(jnp.where(r_id == c_id, square_r, 0.0), axis=0, keepdims=True)
        mixed = jnp.where(r_id < c_id, square_r, jnp.where(r_id > c_id, square_i, 0.0))
        pieces = [(lo, hi, mixed)]
        if lo > 0:
            imag = (
                dot_t(a_i, hband[:, half : half + lo])
                + dot_t(ha_i, band[:, half : half + lo])
                - dot_t(b_i, hband[:, :lo])
                - dot_t(hb_i, band[:, :lo])
            ) * scale
            pieces.append((0, lo, imag))
        if hi < half:
            real = (
                dot_t(a_i, hband[:, hi:half])
                + dot_t(b_i, hband[:, half + hi :])
                + dot_t(ha_i, band[:, hi:half])
                + dot_t(hb_i, band[:, half + hi :])
            ) * scale
            pieces.append((hi, half, real))
        for c0, c1, value in pieces:
            store(i, slice(c0, c1), value)
        return diag

    copies = {}

    def send(c, stage, src, dst, target):
        copies[c, stage] = remote(src, dst, c_send.at[c, stage], c_recv.at[c, stage], target)
        copies[c, stage].start()

    def places(c):
        half_rows, quarter = CHUNK // 2, CHUNK // 4
        if c % PERIOD == PERIOD - 1:
            first, second, near, far = parity, x, pair, across
        else:
            first, second, near, far = x, parity, across, pair
        mine = c * CHUNK + first * half_rows
        other = c * CHUNK + (1 - first) * half_rows
        own = second * quarter
        rest = (1 - second) * quarter
        return mine, other, own, rest, near, far

    def span(start, size):
        return pl.ds(pl.multiple_of(start, 16), size)

    def begin(c):
        mine, other, own, rest, near, far = places(c)
        s1[c] = packed[span(other, CHUNK // 2), :].astype(jnp.bfloat16)
        send(c, 0, s1.at[c], r1.at[c], near)

    def advance(c, stage):
        mine, other, own, rest, near, far = places(c)
        quarter = CHUNK // 4
        copies[c, stage].wait_recv()
        if stage == 0:
            s2[c] = (
                packed[span(mine + rest, quarter), :]
                + r1[c, span(rest, quarter), :].astype(jnp.float32)
            ).astype(jnp.bfloat16)
            send(c, 1, s2.at[c], r2.at[c], far)
            packed[span(mine + own, quarter), :] = packed[span(mine + own, quarter), :] + r1[
                c, span(own, quarter), :
            ].astype(jnp.float32)
        elif stage == 1:
            value = packed[span(mine + own, quarter), :] + r2[c].astype(jnp.float32)
            s3[c] = value.astype(jnp.bfloat16)
            send(c, 2, s3.at[c], r3.at[c], cross)
            packed[span(mine + own, quarter), :] = value
        elif stage == 2:
            value = packed[span(mine + own, quarter), :] + r3[c].astype(jnp.float32)
            ready = full.at[span(mine + own, quarter), :]
            full[span(mine + own, quarter), :] = value.astype(jnp.bfloat16)
            send(c, 3, ready, ready, far)
            send(c, 4, ready, ready, near)
        elif stage == 3:
            ready = full.at[span(mine + rest, quarter), :]
            send(c, 5, ready, ready, near)

    per_tile = TILE // CHUNK
    handed = [
        remote(t_out.at[i], t_in.at[i], t_send.at[i], t_recv.at[i], mate) for i in range(tiles)
    ]

    def store_theirs(i, columns, value):
        t_out[i, :, columns] = value.astype(jnp.bfloat16)

    def store_own(i, columns, value):
        packed[i * TILE : (i + 1) * TILE, columns] = value + t_in[i, :, columns].astype(jnp.float32)

    def hand(i):
        d_out[:, i * TILE : (i + 1) * TILE] = project(nb, nh, i, store_theirs)

    def keep(i):
        handed[i].wait_recv()
        dl[:, i * TILE : (i + 1) * TILE] = project(mb, mh, i, store_own)
        for c in range(i * per_tile, (i + 1) * per_tile):
            begin(c)

    per_tile = TILE // CHUNK
    loads[0].wait()
    loads[1].wait()
    hand(0)
    pl.semaphore_wait(barrier, CHIPS)
    handed[0].start()
    loads[2].wait()
    loads[3].wait()
    for i in range(1, tiles):
        hand(i)
        handed[i].start()
        keep(i - 1)
    swap_d = remote(d_out, d_in, in_send.at[1], in_recv.at[1], mate)
    swap_d.start()
    swap_b = remote(nb, rb, in_send.at[0], in_recv.at[0], mate)
    swap_b.start()
    keep(tiles - 1)
    swap_d.wait()
    dl[...] = dl[...] + d_in[...]
    traces = []
    for r in range(1, CHIPS):
        copy = remote(
            dl,
            dr.at[r - 1],
            ds_sem.at[r - 1],
            dr_sem.at[r - 1],
            device(lax.rem(chip + r, CHIPS), core),
        )
        copy.start()
        traces.append(copy)
    events = sorted(
        (c - (c == count - 2) + LAGS[stage], stage, c) for c in range(count) for stage in range(4)
    )
    for n, (_, stage, c) in enumerate(events):
        advance(c, stage)
        if n == count:
            sum_m[...] = mb[:, :half] + mb[:, half:]
        if n == 2 * count:
            swap_b.wait()
            sum_r[...] = rb[:, :half] + rb[:, half:]
    for c in range(count):
        copies[c, 4].wait_recv()
        copies[c, 5].wait_recv()
    diag = dl[...]
    for r in range(1, CHIPS):
        traces[r - 1].wait()
        diag = diag + dr[r - 1]

    level = jnp.sum(diag, axis=1, keepdims=True) / half
    centred = diag - level
    total = jnp.sum(centred * centred, axis=1, keepdims=True)
    square_sum = jnp.zeros((1, half), jnp.float32)
    for i in range(tiles):
        block = full[i * TILE : (i + 1) * TILE, :].astype(jnp.float32)
        square_sum = square_sum + jnp.sum(block * block, axis=0, keepdims=True)
    total = total + 2.0 * jnp.sum(square_sum, axis=1, keepdims=True)
    spread = jnp.sqrt(total / half + 1e-06)
    factor = 1.0 / (4.0 * spread)
    filling = occ_ref[core].astype(jnp.float32) / half
    on_diag = filling - centred * factor
    for i in range(tiles):
        rows_i = slice(i * TILE, (i + 1) * TILE)
        r_id = lax.broadcasted_iota(jnp.int32, (TILE, TILE), 0)
        c_id = lax.broadcasted_iota(jnp.int32, (TILE, TILE), 1)
        block = full[rows_i, rows_i].astype(jnp.float32) * factor
        turned = block.T
        re0[rows_i, rows_i] = jnp.where(
            r_id == c_id, on_diag[:, rows_i], jnp.where(r_id < c_id, -block, -turned)
        ).astype(jnp.bfloat16)
        im0[rows_i, rows_i] = jnp.where(r_id > c_id, -block, turned).astype(jnp.bfloat16)
        for j in range(i + 1, tiles):
            rows_j = slice(j * TILE, (j + 1) * TILE)
            upper = full[rows_i, rows_j].astype(jnp.float32) * factor
            lower = full[rows_j, rows_i].astype(jnp.float32) * factor
            re0[rows_i, rows_j] = (-upper).astype(jnp.bfloat16)
            re0[rows_j, rows_i] = (-upper.T).astype(jnp.bfloat16)
            im0[rows_j, rows_i] = (-lower).astype(jnp.bfloat16)
            im0[rows_i, rows_j] = lower.T.astype(jnp.bfloat16)

    def three(left, right):
        p = dot(left[0], right[0])
        q = dot(left[1], right[1])
        return p - q, dot(left[2], right[2]) - (p + q)

    def mirror(i, refs, real, imag):
        lo = i * TILE
        real, imag = real.astype(jnp.bfloat16), imag.astype(jnp.bfloat16)
        own_rows, right = slice(lo, lo + TILE), slice(lo, half)
        places = [(own_rows, right, real, imag)]
        for k in range(1, tiles - i):
            part = slice(k * TILE, (k + 1) * TILE)
            below = slice(lo + k * TILE, lo + (k + 1) * TILE)
            places.append((below, own_rows, real[:, part].T, -imag[:, part].T))
        for down, along, r, i in places:
            for ref, value in zip(refs, (r, i, r + i)):
                ref[down, along] = value

    def purify(now, following):
        for i in range(tiles):
            lo = i * TILE
            own_rows = slice(lo, lo + TILE)
            right = slice(lo, half)
            columns = [ref[:, right] for ref in now]
            sq_r, sq_i = three([ref[own_rows, :] for ref in now], columns)
            mirror(i, (sr, si), sq_r, sq_i)
            s_r, s_i = sr[own_rows, :], si[own_rows, :]
            cube_r, cube_i = three([s_r, s_i, s_r + s_i], columns)
            mirror(i, following, 3.0 * sq_r - 2.0 * cube_r, 3.0 * sq_i - 2.0 * cube_i)

    m0[...] = re0[...] + im0[...]
    bufs = [(re0, im0, m0), (re1, im1, m1)]
    for step in range(MCW):
        purify(bufs[step % 2], bufs[(step + 1) % 2])
    last = [ref[...] for ref in bufs[MCW % 2]]

    def update(band, band_sum, target):
        real, imag = three([band[:, :half], band[:, half:], band_sum[...]], last)
        target[:, :half] = real.astype(jnp.bfloat16)
        target[:, half:] = imag.astype(jnp.bfloat16)

    backs = []
    for n in range(2):
        part = slice(n * rows // 2, (n + 1) * rows // 2)
        update(rb.at[part, :], sum_r.at[part, :], ob.at[part, :])
        back = remote(
            ob.at[part, :], out_ref.at[core, part, :], o_send.at[n], o_recv.at[n], mate
        )
        back.start()
        backs.append(back)
    update(mb, sum_m, out_ref.at[core])
    for back in backs:
        back.wait()
    for copy in handed:
        copy.wait_send()
    for copy in copies.values():
        copy.wait_send()


def fused(bands, hbands, occupied):
    points, rows, columns = bands.shape
    half = columns // 2
    count = half // CHUNK
    scale = 1.0 / (2.0 * rows * lax.axis_size("grid"))
    bf16, f32 = jnp.bfloat16, jnp.float32
    dma = pltpu.SemaphoreType.DMA
    return pl.pallas_call(
        functools.partial(kernel, scale),
        out_shape=pltpu.VMEM(bands.shape, bf16),
        in_specs=[
            pl.BlockSpec(memory_space=pltpu.SMEM),
            pl.BlockSpec(memory_space=pltpu.HBM),
            pl.BlockSpec(memory_space=pltpu.HBM),
        ],
        out_specs=pl.BlockSpec(memory_space=pltpu.VMEM),
        scratch_shapes=[
            pltpu.VMEM((rows, columns), bf16),
            pltpu.VMEM((rows, columns), bf16),
            pltpu.VMEM((rows, columns), bf16),
            pltpu.VMEM((rows, columns), bf16),
            pltpu.VMEM((rows, columns), bf16),
            pltpu.VMEM((half // TILE, TILE, half), bf16),
            pltpu.VMEM((half // TILE, TILE, half), bf16),
            pltpu.VMEM((half, half), f32),
            pltpu.VMEM((count, CHUNK // 2, half), bf16),
            pltpu.VMEM((count, CHUNK // 2, half), bf16),
            pltpu.VMEM((count, CHUNK // 4, half), bf16),
            pltpu.VMEM((count, CHUNK // 4, half), bf16),
            pltpu.VMEM((count, CHUNK // 4, half), bf16),
            pltpu.VMEM((count, CHUNK // 4, half), bf16),
            pltpu.VMEM((1, half), f32),
            pltpu.VMEM((1, half), f32),
            pltpu.VMEM((1, half), f32),
            pltpu.VMEM((CHIPS - 1, 1, half), f32),
            pltpu.VMEM((half, half), bf16),
            pltpu.VMEM((half, half), bf16),
            pltpu.VMEM((half, half), bf16),
            pltpu.VMEM((half, half), bf16),
            pltpu.VMEM((half, half), bf16),
            pltpu.VMEM((half, half), bf16),
            pltpu.VMEM((half, half), bf16),
            pltpu.VMEM((half, half), bf16),
            pltpu.VMEM((half, half), bf16),
            pltpu.VMEM((rows, half), bf16),
            pltpu.VMEM((rows, half), bf16),
            pltpu.VMEM((rows, columns), bf16),
            dma((2,)),
            dma((2,)),
            dma((half // TILE,)),
            dma((half // TILE,)),
            dma((CHIPS - 1,)),
            dma((CHIPS - 1,)),
            dma((count, 6)),
            dma((count, 6)),
            dma((2,)),
            dma((2,)),
            dma((4,)),
        ],
        compiler_params=pltpu.CompilerParams(
            collective_id=0, has_side_effects=True, vmem_limit_bytes=40 * 1024 * 1024
        ),
    )(*(pltpu.with_memory_space_constraint(x, pltpu.HBM) for x in (occupied, bands, hbands)))


def embedding(full):
    width = full.shape[-1] // 2
    real_part = full[..., :width]
    imag_part = full[..., width:]
    upper = jnp.concatenate([real_part, imag_part], -1)
    lower = jnp.concatenate([-imag_part, real_part], -1)
    return jnp.concatenate([upper, lower], -2)


def spread_out(bands, hbands, occupied):
    points, local_rows, columns = bands.shape
    half = columns // 2
    devices = lax.axis_size("grid")
    share = half // devices
    scale = 1.0 / (2.0 * local_rows * devices)
    blocks = []
    for point in range(points):
        start = jnp.int32(0)
        count = lax.axis_size("grid") * share
        band_k = bands[point]
        hband_k = hbands[point]
        band_cols = jnp.concatenate(
            [
                lax.dynamic_slice_in_dim(band_k, start, count, 1),
                lax.dynamic_slice_in_dim(band_k, half, count, 1),
            ],
            1,
        )
        summed = jnp.einsum("gi,gj->ij", band_cols, hband_k, preferred_element_type=jnp.float32)
        hband_cols = jnp.concatenate(
            [
                lax.dynamic_slice_in_dim(hband_k, start, count, 1),
                lax.dynamic_slice_in_dim(hband_k, half, count, 1),
            ],
            1,
        )
        summed = summed + jnp.einsum(
            "gi,gj->ij", hband_cols, band_k, preferred_element_type=jnp.float32
        )
        real_rows = (summed[:count, :half] + summed[count:, half:]) * scale
        imag_rows = (summed[:count, half:] - summed[count:, :half]) * scale
        blocks.append(
            lax.psum_scatter(
                jnp.concatenate([real_rows, imag_rows], 1), "grid", scatter_dimension=0, tiled=True
            )
        )
    hamiltonian = jnp.stack(blocks, 1)
    hamiltonian = jnp.transpose(hamiltonian, (1, 0, 2))
    ham_real = hamiltonian[:, :, :half]
    ham_imag = hamiltonian[:, :, half:]
    row_index = lax.axis_index("grid") * share + lax.iota(jnp.int32, share)
    col_index = lax.iota(jnp.int32, half)
    identity = (row_index[:, None] == col_index[None, :]).astype(jnp.float32)[None]
    trace_part = jnp.sum(ham_real * identity, axis=(1, 2))
    trace = lax.psum(trace_part, "grid")
    level = (trace / half)[:, None, None]
    centred = ham_real - level * identity
    squares = jnp.sum(centred * centred, axis=(1, 2)) + jnp.sum(ham_imag * ham_imag, axis=(1, 2))
    total = lax.psum(squares, "grid")
    spread = jnp.sqrt(total / half + 1e-06)[:, None, None]
    filling = (occupied.astype(jnp.float32) / half)[:, None, None]
    dens_real = filling * identity - centred / (4.0 * spread)
    dens_imag = -ham_imag / (4.0 * spread)
    density = jnp.concatenate([dens_real, dens_imag], 2).astype(jnp.bfloat16)
    for repeat in range(MCW):
        gathered = lax.all_gather(density, "grid", axis=1, tiled=True)
        matrix = embedding(gathered)
        square = jnp.einsum("krc,kcd->krd", density, matrix, preferred_element_type=jnp.float32)
        cube = jnp.einsum(
            "krc,kcd->krd", square.astype(jnp.bfloat16), matrix, preferred_element_type=jnp.float32
        )
        density = (3.0 * square - 2.0 * cube).astype(jnp.bfloat16)
    gathered = lax.all_gather(density, "grid", axis=1, tiled=True)
    matrix = embedding(gathered)
    updated = jnp.einsum("kgc,kcd->kgd", bands, matrix, preferred_element_type=jnp.float32)
    return updated.astype(jnp.bfloat16)


def on_device(bands, hbands, occupied):
    points, rows, columns = bands.shape
    half = columns // 2
    if (
        lax.axis_size("grid") == 2 * CHIPS
        and points == 2
        and half % TILE == 0
        and half % (16 * CHIPS) == 0
    ):
        return fused(bands, hbands, occupied)
    return spread_out(bands, hbands, occupied)


def solution(mesh):
    return jax.shard_map(
        on_device,
        mesh=mesh,
        in_specs=(P("kset", "grid", None), P("kset", "grid", None), P("kset")),
        out_specs=P("kset", "grid", None),
        check_vma=False,
    )
```
